32 devices in a mesh: grp: 2 (over y), comp: 4 (over z), space: 4 (over x, core).
Axes of the slice: x: 2, y: 2, z: 4, core: 2. Of those that a mesh axis runs over, the one named last changes fastest.
Arguments:
- spectrum: float32 [2304, 4096], P('comp', ('grp', 'space')), parts along dimension 1, may hold values from -6 to 6
- wave_speed: float32 [36], replicated, may hold values from 0.25 to 2
- current_east: float32 [4096], P(('grp', 'space')), parts along dimension 0, may hold values from -3 to 3
- current_north: float32 [4096], P(('grp', 'space')), parts along dimension 0, may hold values from -3 to 3
- substeps: int32 [2304], replicated, may hold values from 1 to 4, as said below
- neighbours: int32 [4, 4096], P(None, ('grp', 'space')), parts along dimension 1, may hold values from 0 to 767, as said below
- blocks: bfloat16 [64, 64, 64], replicated, may hold values from -0.75 to 0.75
- quad_index: int32 [4, 64], replicated, may hold values from 0 to 35
- strength: float32 [64], replicated, may hold values from -1 to 1
Outputs:
- spectrum_out: float32 [2304, 4096], P('comp', ('grp', 'space')), parts along dimension 1
The draws below stay inside these ranges and needn't reach their ends.
There are 2 independent parts, one for each index of `grp`. The reference program is written for one: setup_inputs(seed, part) draws one part's arguments, and reference() takes and returns one part's arrays. A program takes and returns all parts, laid end to end along the dimension named above; an argument that names none is the same for every part. Nothing has to cross between parts.
Inputs may be any that keep to these rules, and one draw needn't show every extreme that they name: `substeps`: component 0 takes 4. `neighbours`: the entry of row r for the slab's point q (counted within its slab) is q + 128 + o, with -128 <= o <= -1 for rows 0 and 2 and 1 <= o <= 128 for rows 1 and 3.
All inputs are finite; a program needn't handle non-finite values.
Results may differ from the reference program's by a relative error of at most 0.00031.
Values sent between devices are 32-bit elements; how exact they have to be, the bound alone decides.
A program may use at most 64 MiB of HBM per device.

```python
import math
import jax
import jax.numpy as jnp
from jax import lax

NF = 36
ND = 64
NBLK = 64
SUB = 4
HALO = 128
STEPS = 1
K = 2304
PTS_SLAB = 512
PTS = 2048


def draw_substeps(key, part):
    components = jnp.arange(NF * ND, dtype=jnp.int32)
    frequency = components // ND
    jitter = jax.random.randint(key, (NF * ND,), -1, 1, dtype=jnp.int32)
    counts = SUB - frequency * SUB // NF + jitter
    counts = jnp.clip(counts, 1, SUB)
    return counts.at[0].set(SUB).astype(jnp.int32)


def draw_neighbours(key, part):
    offsets = jax.random.randint(key, (4, PTS), 1, HALO + 1, dtype=jnp.int32)
    direction_sign = jnp.array([-1, 1, -1, 1], dtype=jnp.int32)[:, None]
    position = (jnp.arange(PTS, dtype=jnp.int32) % PTS_SLAB)[None, :]
    row_number = jnp.arange(4, dtype=jnp.int32)[:, None]
    extended = position + HALO + direction_sign * offsets
    extended = jnp.where((row_number == 0) & (position == 0), 0, extended)
    extended = jnp.where((row_number == 1) & (position == PTS_SLAB - 1), PTS_SLAB + 2 * HALO - 1, extended)
    return extended.astype(jnp.int32)


def draw_quad_index(key, part):
    table = jax.random.randint(key, (4, NBLK), 0, NF, dtype=jnp.int32)
    table = table.at[:, 0].set(0)
    table = table.at[:, 1].set(NF - 1)
    return table.astype(jnp.int32)


def shard_levels(own_key, extent, shards, least, high):
    level, own = 1.0, jax.random.fold_in(own_key, 6)
    for dim, shards_of in shards:
        steps = jnp.exp(jax.random.uniform(jax.random.fold_in(own, dim), (shards_of,), jnp.float32, least / len(shards), high / len(shards)))
        level = level * jnp.repeat(steps, extent[dim] // shards_of).reshape([-1 if axis == dim else 1 for axis in range(len(extent))])
    return level


def scatter_about(rng, extent, deviation, bound, cuts=(), held_as=jnp.bfloat16):
    result = deviation * jax.random.normal(rng, extent, jnp.float32)
    if cuts:
        result = result * shard_levels(rng, extent, cuts, -0.22, 0.18)
    return jnp.clip(result, -bound, bound).astype(held_as)


def setup_inputs(seed: int = 0, part: int = 0) -> dict:
    key_of = jax.random.split(jax.random.key(seed), 10)
    part_splits = jax.random.split(jax.random.fold_in(key_of[9], part), 10)
    return {
        "spectrum": scatter_about(part_splits[0], (K, PTS), 1.0, 6.0, ((0, 4), (1, 4)), jnp.float32),
        "wave_speed": jnp.clip(jnp.exp(jax.random.uniform(key_of[1], (NF,), jnp.float32, math.log(0.25), math.log(2.0))), 0.25, 2.0),
        "current_east": scatter_about(part_splits[2], (PTS,), 0.5, 3.0, ((0, 4),), jnp.float32),
        "current_north": scatter_about(part_splits[3], (PTS,), 0.5, 3.0, ((0, 4),), jnp.float32),
        "substeps": draw_substeps(jax.random.fold_in(key_of[9], 71), part),
        "neighbours": draw_neighbours(jax.random.fold_in(jax.random.fold_in(key_of[9], part), 71), part),
        "blocks": scatter_about(key_of[6], (NBLK, ND, ND), ND ** -0.5, 0.75),
        "quad_index": draw_quad_index(jax.random.fold_in(key_of[9], 71), part),
        "strength": jnp.clip(jax.random.uniform(key_of[8], (NBLK,), jnp.float32, -1.0, 1.0), -1.0, 1.0),
    }


courant_scale = 0.4
courant_limit = 0.45
source_step = 0.1


def reference(spectrum, wave_speed, current_east, current_north, substeps, neighbours, blocks, quad_index, strength):
    global_index = (jnp.arange(PTS, dtype=jnp.int32) // PTS_SLAB) * PTS_SLAB + neighbours
    angles = (jnp.arange(ND, dtype=jnp.float32) + 0.5) * (2.0 * math.pi / ND)

    def per_frequency(members):
        values, speed_value, counts = members
        divisor = counts.astype(jnp.float32)[:, None]
        along_x = jnp.clip(((speed_value * jnp.cos(angles))[:, None] + current_east[None, :]) * courant_scale / divisor, -courant_limit, courant_limit)
        along_y = jnp.clip(((speed_value * jnp.sin(angles))[:, None] + current_north[None, :]) * courant_scale / divisor, -courant_limit, courant_limit)
        pos_x = jnp.maximum(along_x, 0.0)
        neg_x = jnp.minimum(along_x, 0.0)
        pos_y = jnp.maximum(along_y, 0.0)
        neg_y = jnp.minimum(along_y, 0.0)
        for repeat in range(SUB):
            padded = jnp.pad(values, ((0, 0), (HALO, HALO)))
            west_value = padded[:, global_index[0]]
            east_value = padded[:, global_index[1]]
            south_value = padded[:, global_index[2]]
            north_value = padded[:, global_index[3]]
            updated = values - pos_x * (values - west_value) - neg_x * (east_value - values) - pos_y * (values - south_value) - neg_y * (north_value - values)
            values = jnp.where(repeat < counts[:, None], updated, values)
        return values

    def propagate(spectra):
        shaped = spectra.reshape(NF, ND, PTS)
        moved = lax.map(per_frequency, (shaped, wave_speed, substeps.reshape(NF, ND)))
        return moved.reshape(NF * ND, PTS)

    def source_term(spectra):
        spectra_grid = spectra.reshape(NF, ND, PTS)
        rounded = spectra_grid.astype(jnp.bfloat16)

        def accumulate(total, index):
            matrix = blocks[index].astype(jnp.float32)
            first_freq = quad_index[0, index]
            second_freq = quad_index[1, index]
            third_freq = quad_index[2, index]
            target = quad_index[3, index]
            left_term = jnp.dot(matrix, rounded[first_freq].astype(jnp.float32), precision=lax.Precision.HIGHEST)
            right_term = jnp.dot(matrix.T, rounded[second_freq].astype(jnp.float32), precision=lax.Precision.HIGHEST)
            product = (left_term * right_term * spectra_grid[third_freq]).astype(jnp.bfloat16)
            part_term = jnp.dot(matrix, product.astype(jnp.float32), precision=lax.Precision.HIGHEST)
            return total.at[target].add(strength[index] * part_term), None

        total, unused = lax.scan(accumulate, jnp.zeros((NF, ND, PTS), jnp.float32), jnp.arange(NBLK, dtype=jnp.int32))
        return (spectra_grid + source_step * total).reshape(NF * ND, PTS)

    spectra = spectrum
    for repeat in range(STEPS):
        spectra = source_term(propagate(spectra))
    return spectra
```

```python
import functools
import math

import jax
import jax.numpy as jnp
import numpy as np
from jax import lax
from jax.experimental import pallas as pl
from jax.experimental.pallas import tpu as pltpu
from jax.sharding import PartitionSpec as P

NF = 36
ND = 64
SUB = 4
HALO = 128

courant_scale = 0.4
courant_limit = 0.45
source_step = 0.1

MESH = pl.DeviceIdType.MESH


def chunk_rows(rows):
    for size in (32, 24, 16, 8):
        if rows % size == 0:
            return size
    return rows


def sync(peers, spaces):
    me = lax.axis_index("comp")
    here = lax.axis_index("space")
    barrier = pltpu.get_barrier_semaphore()
    count = 0
    for k in range(1, peers):
        pl.semaphore_signal(
            barrier, inc=1, device_id={"comp": lax.rem(me + k, peers)}, device_id_type=MESH
        )
        count += 1
    if spaces:
        for k in (1, spaces - 1):
            pl.semaphore_signal(
                barrier, inc=1, device_id={"space": lax.rem(here + k, spaces)}, device_id_type=MESH
            )
            count += 1
    pl.semaphore_wait(barrier, count)


GATHER = lax.GatherDimensionNumbers(
    offset_dims=(),
    collapsed_slice_dims=(1,),
    start_index_map=(1,),
    operand_batching_dims=(0,),
    start_indices_batching_dims=(0,),
)


def take_lanes(values, index):
    return lax.gather(
        values,
        index[:, :, None],
        GATHER,
        slice_sizes=(1, 1),
        mode=lax.GatherScatterMode.PROMISE_IN_BOUNDS,
    )


def propagate_kernel(
    peers,
    spaces,
    chunk,
    block,
    field_ref,
    wave_ref,
    substeps_ref,
    trig_ref,
    east_ref,
    north_ref,
    neighbour_ref,
    points_ref,
    extended,
    finals,
    side_table,
    side_current,
    codes,
    currents,
    load_sem,
    side_send,
    side_recv,
    halo_send,
    halo_recv,
    piece_send,
    piece_recv,
    own_sem,
    turn_sem,
):
    me = lax.axis_index("comp")
    here = lax.axis_index("space")
    rows, width = field_ref.shape
    tiles = width // HALO
    reach = SUB * HALO
    chunks = rows // chunk
    has_left = here > 0
    has_right = here < spaces - 1
    odd = lax.rem(here, 2)
    goes_first = odd == jnp.where(here < spaces // 2, 0, 1)

    load = pltpu.make_async_copy(field_ref, extended.at[:, pl.ds(reach, width)], load_sem)
    load.start()

    sync(peers, spaces)

    left = {"space": jnp.maximum(here - 1, 0)}
    right = {"space": jnp.minimum(here + 1, spaces - 1)}

    def remote(source, target, send, recv, device):
        return pltpu.make_async_remote_copy(
            src_ref=source,
            dst_ref=target,
            send_sem=send,
            recv_sem=recv,
            device_id=device,
            device_id_type=MESH,
        )

    def sides():
        copies = []
        for side, start, device in ((1, 0, left), (0, width - reach, right)):
            part = pl.ds(start, reach)
            pairs = (
                (neighbour_ref.at[:, part], side_table.at[side]),
                (east_ref.at[:, part], side_current.at[side, 0]),
                (north_ref.at[:, part], side_current.at[side, 1]),
            )
            copies.append(
                [
                    remote(source, target, side_send.at[side, i], side_recv.at[side, i], device)
                    for i, (source, target) in enumerate(pairs)
                ]
            )
        return copies

    def halo(first, count, sem):
        part = pl.ds(first, count)
        to_left = remote(
            field_ref.at[part, pl.ds(0, reach)],
            extended.at[part, pl.ds(reach + width, reach)],
            halo_send.at[1],
            halo_recv.at[1, sem],
            left,
        )
        to_right = remote(
            field_ref.at[part, pl.ds(width - reach, reach)],
            extended.at[part, pl.ds(0, reach)],
            halo_send.at[0],
            halo_recv.at[0, sem],
            right,
        )
        return to_left, to_right

    def rows_of(c):
        return pl.multiple_of(c * chunk, 8)

    to_left_sides, to_right_sides = sides()

    @pl.when(has_left)
    def _():
        for copy in to_left_sides:
            copy.start()

    @pl.when(has_right)
    def _():
        for copy in to_right_sides:
            copy.start()

    def start_halo(c, carry):
        to_left, to_right = halo(rows_of(c), chunk, c)

        @pl.when(has_left)
        def _():
            to_left.start()

        @pl.when(has_right)
        def _():
            to_right.start()

        return carry

    lax.fori_loop(0, chunks, start_halo, 0)

    lane = lax.broadcasted_iota(jnp.int32, (4, HALO), 1)
    for side, missing in ((0, jnp.logical_not(has_left)), (1, jnp.logical_not(has_right))):

        @pl.when(missing)
        def _(side=side):
            first = (tiles - SUB) * HALO if side == 0 else 0
            for i in range(SUB):
                part = pl.ds(i * HALO, HALO)
                side_table[side, :, part] = lane + (first + (i + 1) * HALO)
            side_current[side] = jnp.zeros((2, 1, reach), jnp.float32)
            start = 0 if side == 0 else reach + width

            def clear(g, carry):
                at = pl.ds(pl.multiple_of(g * 8, 8), 8)
                extended[at, pl.ds(start, reach)] = jnp.zeros((8, reach), jnp.float32)
                return carry

            lax.fori_loop(0, rows // 8, clear, 0)

    def spread(row):
        return jnp.broadcast_to(row, (8, HALO))

    def fill(e, table_ref, east_row, north_row, tile, place):
        for d in range(4):
            codes[d, e] = spread(table_ref[d : d + 1, place] - tile * HALO)
        currents[0, e] = spread(east_row[:, place])
        currents[1, e] = spread(north_row[:, place])

    def fill_own(j, carry):
        fill(j + SUB, neighbour_ref, east_ref, north_ref, j, pl.ds(pl.multiple_of(j * HALO, HALO), HALO))
        return carry

    lax.fori_loop(0, tiles, fill_own, 0)

    @pl.when(has_right)
    def _():
        for copy in to_left_sides:
            copy.wait_recv()

    @pl.when(has_left)
    def _():
        for copy in to_right_sides:
            copy.wait_recv()

    for i in range(SUB):
        place = pl.ds(i * HALO, HALO)
        fill(i, side_table.at[0], side_current.at[0, 0], side_current.at[0, 1], tiles - SUB + i, place)
        fill(
            SUB + tiles + i, side_table.at[1], side_current.at[1, 0], side_current.at[1, 1], i, place
        )

    sublane = lax.broadcasted_iota(jnp.int32, (8, HALO), 0)
    window = block + 2 * SUB

    def upwind(before, own, after, code, index):
        picked = jnp.where(code >= 2 * HALO, take_lanes(after, index), take_lanes(own, index))
        return jnp.where(code < HALO, take_lanes(before, index), picked)

    def strip(row, b):
        at = pl.ds(row, 8)
        component = me * rows + row
        speed = wave_ref[component // ND]
        turn = pl.ds(pl.multiple_of(lax.rem(component, ND), 8), 8)
        own_x = trig_ref[0, turn, :] * speed
        own_y = trig_ref[1, turn, :] * speed
        taken = jnp.full((8, HALO), substeps_ref[component], jnp.int32)
        for i in range(1, 8):
            taken = jnp.where(sublane == i, substeps_ref[component + i], taken)
        scale = courant_scale / taken.astype(jnp.float32)
        base = b * block
        values = [
            extended[at, pl.ds(pl.multiple_of((base + i) * HALO, HALO), HALO)] for i in range(window)
        ]
        along = {}
        for i in range(1, window - 1):
            entry = []
            for axis, own in ((0, own_x), (1, own_y)):
                moved = (own + currents[axis, base + i]) * scale
                moved = jnp.clip(moved, -courant_limit, courant_limit)
                code = jnp.where(moved > 0.0, codes[2 * axis, base + i], codes[2 * axis + 1, base + i])
                entry.append((jnp.abs(moved), code, jnp.bitwise_and(code, HALO - 1)))
            along[i] = entry
        for s in range(SUB):
            latest = list(values)
            for i in range(s + 1, window - 1 - s):
                own = values[i]
                change = None
                for size, code, index in along[i]:
                    term = size * (own - upwind(values[i - 1], own, values[i + 1], code, index))
                    change = term if change is None else change + term
                if s > 0:
                    change = jnp.where(taken > s, change, 0.0)
                latest[i] = own - change
            values = latest
        for i in range(block):
            finals[base + i, at] = values[SUB + i]

    def piece(k, first, count):
        target = lax.rem(me + k, peers)
        return remote(
            finals.at[target, pl.ds(first, count)],
            points_ref.at[pl.ds(pl.multiple_of(me * rows + first, 8), count)],
            piece_send.at[k],
            piece_recv.at[k],
            {"comp": target},
        )

    order = sorted(range(1, peers), key=lambda k: abs(k - peers / 2))
    load.wait()

    def step(c, carry):
        first = rows_of(c)
        to_left, to_right = halo(first, chunk, c)

        @pl.when(has_right)
        def _():
            to_left.wait_recv()

        @pl.when(has_left)
        def _():
            to_right.wait_recv()

        def per_strip(g, inner):
            row = pl.multiple_of(first + g * 8, 8)

            def per_block(b, deepest):
                strip(row, b)
                return deepest

            if tiles == block:
                strip(row, 0)
                return inner
            return lax.fori_loop(0, tiles // block, per_block, inner)

        lax.fori_loop(0, chunk // 8, per_strip, 0)

        @pl.when(goes_first)
        def _():
            for k in order:
                piece(k, first, chunk).start()

        return carry

    lax.fori_loop(0, chunks, step, 0)
    own = pltpu.make_async_copy(
        finals.at[me], points_ref.at[pl.ds(pl.multiple_of(me * rows, 8), rows)], own_sem
    )
    own.start()

    @pl.when(jnp.logical_not(goes_first))
    def _():
        pl.semaphore_wait(turn_sem, 1)
        for k in order:
            piece(k, 0, rows).start()

    for k in order:
        piece(k, 0, rows).wait_send()

    @pl.when(goes_first)
    def _():
        partner = here + 1 - 2 * odd
        pl.semaphore_signal(turn_sem, inc=1, device_id={"space": partner}, device_id_type=MESH)

    own.wait()
    to_left, to_right = halo(0, rows, 0)

    @pl.when(has_left)
    def _():
        to_left.wait_send()
        for copy in to_left_sides:
            copy.wait_send()

    @pl.when(has_right)
    def _():
        to_right.wait_send()
        for copy in to_right_sides:
            copy.wait_send()

    for k in order:
        piece(k, 0, rows).wait_recv()


def propagate(field, wave_speed, substeps, east, north, neighbours, peers, spaces):
    rows, width = field.shape
    tiles = width // HALO
    reach = SUB * HALO
    assert width >= reach and spaces % 2 == 0
    chunk = chunk_rows(rows)
    block = math.gcd(tiles, 4)
    outer = tiles + 2 * SUB
    angles = (np.arange(ND, dtype=np.float32) + np.float32(0.5)) * np.float32(2.0 * math.pi / ND)
    trig = np.stack([np.cos(angles), np.sin(angles)])
    trig = np.ascontiguousarray(np.broadcast_to(trig[:, :, None], (2, ND, HALO)))
    vmem = pl.BlockSpec(memory_space=pltpu.VMEM)
    smem = pl.BlockSpec(memory_space=pltpu.SMEM)
    return pl.pallas_call(
        functools.partial(propagate_kernel, peers, spaces, chunk, block),
        out_shape=jax.ShapeDtypeStruct((peers * rows, HALO), jnp.float32),
        in_specs=[pl.BlockSpec(memory_space=pl.ANY), smem, smem, vmem, vmem, vmem, vmem],
        out_specs=vmem,
        scratch_shapes=[
            pltpu.VMEM((rows, width + 2 * reach), jnp.float32),
            pltpu.VMEM((tiles, rows, HALO), jnp.float32),
            pltpu.VMEM((2, 4, reach), jnp.int32),
            pltpu.VMEM((2, 2, 1, reach), jnp.float32),
            pltpu.VMEM((4, outer, 8, HALO), jnp.int32),
            pltpu.VMEM((2, outer, 8, HALO), jnp.float32),
            pltpu.SemaphoreType.DMA,
            pltpu.SemaphoreType.DMA((2, 3)),
            pltpu.SemaphoreType.DMA((2, 3)),
            pltpu.SemaphoreType.DMA((2,)),
            pltpu.SemaphoreType.DMA((2, rows // chunk)),
            pltpu.SemaphoreType.DMA((peers,)),
            pltpu.SemaphoreType.DMA((peers,)),
            pltpu.SemaphoreType.DMA,
            pltpu.SemaphoreType.REGULAR,
        ],
        compiler_params=pltpu.CompilerParams(collective_id=0, has_side_effects=True),
    )(
        field,
        wave_speed,
        substeps,
        jnp.asarray(trig),
        east.reshape(1, width),
        north.reshape(1, width),
        neighbours,
    )


def source_kernel(batch, quad_ref, strength_ref, points_ref, blocks_ref, out_ref, rounded, products):
    total = blocks_ref.shape[0]

    def fill(f, carry):
        value = points_ref[f]
        rounded[f] = value.astype(jnp.bfloat16)
        out_ref[f] = value
        return carry

    lax.fori_loop(0, NF, fill, 0, unroll=4)

    def step(i, carry):
        for b in range(batch):
            j = i * batch + b
            block = blocks_ref[j]
            left = jnp.dot(block, rounded[quad_ref[0, j]], preferred_element_type=jnp.float32)
            right = lax.dot_general(
                block,
                rounded[quad_ref[1, j]],
                (((0,), (0,)), ((), ())),
                preferred_element_type=jnp.float32,
            )
            products[b] = (left * right * points_ref[quad_ref[2, j]]).astype(jnp.bfloat16)
        parts = []
        for b in range(batch):
            j = i * batch + b
            part = jnp.dot(blocks_ref[j], products[b], preferred_element_type=jnp.float32)
            parts.append(part * (strength_ref[j] * source_step))
        for b in range(batch):
            target = quad_ref[3, i * batch + b]
            out_ref[target] = out_ref[target] + parts[b]
        return carry

    lax.fori_loop(0, total // batch, step, 0)


def source_term(points, blocks, quad_index, strength):
    width = points.shape[1]
    vmem = pl.BlockSpec(memory_space=pltpu.VMEM)
    smem = pl.BlockSpec(memory_space=pltpu.SMEM)
    batch = math.gcd(blocks.shape[0], 32)
    out = pl.pallas_call(
        functools.partial(source_kernel, batch),
        out_shape=jax.ShapeDtypeStruct((NF, ND, width), jnp.float32),
        in_specs=[smem, smem, vmem, vmem],
        out_specs=vmem,
        scratch_shapes=[
            pltpu.VMEM((NF, ND, width), jnp.bfloat16),
            pltpu.VMEM((batch, ND, width), jnp.bfloat16),
        ],
    )(quad_index, strength, points.reshape(NF, ND, width), blocks)
    return out.reshape(NF * ND, width)


def home_kernel(peers, points_ref, out_ref, send_sem, recv_sem, own_sem):
    me = lax.axis_index("comp")
    rows = out_ref.shape[0]
    place = pl.ds(pl.multiple_of(me * HALO, HALO), HALO)
    own = pltpu.make_async_copy(
        points_ref.at[pl.ds(pl.multiple_of(me * rows, 8), rows)], out_ref.at[:, place], own_sem
    )
    own.start()
    sync(peers, 0)
    copies = []
    for k in sorted(range(1, peers), key=lambda k: abs(k - peers / 2)):
        target = lax.rem(me + k, peers)
        copy = pltpu.make_async_remote_copy(
            src_ref=points_ref.at[pl.ds(pl.multiple_of(target * rows, 8), rows)],
            dst_ref=out_ref.at[:, place],
            send_sem=send_sem.at[k],
            recv_sem=recv_sem.at[k],
            device_id={"comp": target},
            device_id_type=MESH,
        )
        copy.start()
        copies.append(copy)
    own.wait()
    for copy in copies:
        copy.wait()


def send_home(points, peers):
    rows = points.shape[0] // peers
    return pl.pallas_call(
        functools.partial(home_kernel, peers),
        out_shape=jax.ShapeDtypeStruct((rows, peers * HALO), jnp.float32),
        in_specs=[pl.BlockSpec(memory_space=pltpu.VMEM)],
        out_specs=pl.BlockSpec(memory_space=pltpu.VMEM),
        scratch_shapes=[
            pltpu.SemaphoreType.DMA((peers,)),
            pltpu.SemaphoreType.DMA((peers,)),
            pltpu.SemaphoreType.DMA,
        ],
        compiler_params=pltpu.CompilerParams(collective_id=1, has_side_effects=True),
    )(points)


def shards(
    spectrum,
    wave_speed,
    current_east,
    current_north,
    substeps,
    neighbours,
    blocks,
    quad_index,
    strength,
):
    peers = lax.axis_size("comp")
    spaces = lax.axis_size("space")
    rows, width = spectrum.shape
    assert width == peers * HALO
    points = propagate(
        spectrum, wave_speed, substeps, current_east, current_north, neighbours, peers, spaces
    )
    points = source_term(points, blocks, quad_index, strength)
    return send_home(points, peers)


def solution(mesh):
    in_specs = (
        P("comp", ("grp", "space")),
        P(),
        P(("grp", "space")),
        P(("grp", "space")),
        P(),
        P(None, ("grp", "space")),
        P(),
        P(),
        P(),
    )
    out_specs = P("comp", ("grp", "space"))
    return jax.shard_map(shards, mesh=mesh, in_specs=in_specs, out_specs=out_specs, check_vma=False)
```

```python
import functools
import math

import jax
import jax.numpy as jnp
import numpy as np
from jax import lax
from jax.experimental import pallas as pl
from jax.experimental.pallas import tpu as pltpu
from jax.sharding import PartitionSpec as P

NF = 36
ND = 64
SUB = 4
HALO = 128
PARTS = 2

courant_scale = 0.4
courant_limit = 0.45
source_step = 0.1

MESH = pl.DeviceIdType.MESH


def chunk_rows(rows):
    for size in (64, 72, 48, 32, 24, 16, 8):
        if rows % size == 0:
            return size
    return rows


def sync(peers, spaces):
    me = lax.axis_index("comp")
    here = lax.axis_index("space")
    barrier = pltpu.get_barrier_semaphore()
    count = 0
    for k in range(1, peers):
        pl.semaphore_signal(
            barrier, inc=1, device_id={"comp": lax.rem(me + k, peers)}, device_id_type=MESH
        )
        count += 1
    if spaces:
        for k in (1, spaces - 1):
            pl.semaphore_signal(
                barrier, inc=1, device_id={"space": lax.rem(here + k, spaces)}, device_id_type=MESH
            )
            count += 1
    pl.semaphore_wait(barrier, count)


def propagate_kernel(
    peers,
    spaces,
    chunk,
    block,
    field_ref,
    wave_ref,
    substeps_ref,
    trig_ref,
    east_ref,
    north_ref,
    neighbour_ref,
    points_ref,
    extended,
    finals,
    side_table,
    side_current,
    selector,
    currents,
    states,
    parts,
    speeds,
    repeats,
    load_sem,
    side_send,
    side_recv,
    halo_send,
    halo_recv,
    piece_send,
    piece_recv,
    own_sem,
    turn_sem,
):
    me = lax.axis_index("comp")
    here = lax.axis_index("space")
    rows, width = field_ref.shape
    tiles = width // HALO
    reach = SUB * HALO
    chunks = rows // chunk
    has_left = here > 0
    has_right = here < spaces - 1
    odd = lax.rem(here, 2)
    goes_first = odd == jnp.where(here < spaces // 2, 0, 1)

    load = pltpu.make_async_copy(field_ref, extended.at[:, pl.ds(reach, width)], load_sem)
    load.start()

    sync(peers, spaces)

    left = {"space": jnp.maximum(here - 1, 0)}
    right = {"space": jnp.minimum(here + 1, spaces - 1)}

    def remote(source, target, send, recv, device):
        return pltpu.make_async_remote_copy(
            src_ref=source,
            dst_ref=target,
            send_sem=send,
            recv_sem=recv,
            device_id=device,
            device_id_type=MESH,
        )

    def sides():
        copies = []
        for side, start, device in ((1, 0, left), (0, width - reach, right)):
            part = pl.ds(start, reach)
            pairs = (
                (neighbour_ref.at[:, part], side_table.at[side]),
                (east_ref.at[:, part], side_current.at[side, 0]),
                (north_ref.at[:, part], side_current.at[side, 1]),
            )
            copies.append(
                [
                    remote(source, target, side_send.at[side, i], side_recv.at[side, i], device)
                    for i, (source, target) in enumerate(pairs)
                ]
            )
        return copies

    def halo(first, count, sem):
        part = pl.ds(first, count)
        to_left = remote(
            field_ref.at[part, pl.ds(0, reach)],
            extended.at[part, pl.ds(reach + width, reach)],
            halo_send.at[1],
            halo_recv.at[1, sem],
            left,
        )
        to_right = remote(
            field_ref.at[part, pl.ds(width - reach, reach)],
            extended.at[part, pl.ds(0, reach)],
            halo_send.at[0],
            halo_recv.at[0, sem],
            right,
        )
        return to_left, to_right

    def rows_of(c):
        return pl.multiple_of(c * chunk, 8)

    to_left_sides, to_right_sides = sides()

    @pl.when(has_left)
    def _():
        for copy in to_left_sides:
            copy.start()

    @pl.when(has_right)
    def _():
        for copy in to_right_sides:
            copy.start()

    def start_halo(c, carry):
        to_left, to_right = halo(rows_of(c), chunk, c)

        @pl.when(has_left)
        def _():
            to_left.start()

        @pl.when(has_right)
        def _():
            to_right.start()

        return carry

    lax.fori_loop(0, chunks, start_halo, 0)

    lane = lax.broadcasted_iota(jnp.int32, (4, HALO), 1)
    for side, missing in ((0, jnp.logical_not(has_left)), (1, jnp.logical_not(has_right))):

        @pl.when(missing)
        def _(side=side):
            first = (tiles - SUB) * HALO if side == 0 else 0
            for i in range(SUB):
                part = pl.ds(i * HALO, HALO)
                side_table[side, :, part] = lane + (first + (i + 1) * HALO)
            side_current[side] = jnp.zeros((2, 1, reach), jnp.float32)
            start = 0 if side == 0 else reach + width

            def clear(g, carry):
                at = pl.ds(pl.multiple_of(g * 8, 8), 8)
                extended[at, pl.ds(start, reach)] = jnp.zeros((8, reach), jnp.float32)
                return carry

            lax.fori_loop(0, rows // 8, clear, 0)

    def spread(row):
        return jnp.broadcast_to(row, (8, HALO))

    spot = lax.broadcasted_iota(jnp.int32, (2 * HALO, HALO), 0)

    def fill(e, table_ref, east_row, north_row, tile, place):
        for d in range(4):
            wanted = table_ref[d : d + 1, place] - (tile + d % 2) * HALO
            half = d // 2 * HALO
            chosen = jnp.where(spot == wanted, 1.0, 0.0).astype(jnp.bfloat16)
            selector[e, d % 2, :, half : half + HALO] = chosen
        currents[0, e] = spread(east_row[:, place])
        currents[1, e] = spread(north_row[:, place])

    def fill_own(j, carry):
        fill(j + SUB, neighbour_ref, east_ref, north_ref, j, pl.ds(pl.multiple_of(j * HALO, HALO), HALO))
        return carry

    lax.fori_loop(0, tiles, fill_own, 0)

    @pl.when(has_right)
    def _():
        for copy in to_left_sides:
            copy.wait_recv()

    @pl.when(has_left)
    def _():
        for copy in to_right_sides:
            copy.wait_recv()

    for i in range(SUB):
        place = pl.ds(i * HALO, HALO)
        fill(i, side_table.at[0], side_current.at[0, 0], side_current.at[0, 1], tiles - SUB + i, place)
        fill(
            SUB + tiles + i, side_table.at[1], side_current.at[1, 0], side_current.at[1, 1], i, place
        )

    sublane = lax.broadcasted_iota(jnp.int32, (8, HALO), 0)
    window = block + 2 * SUB

    def prepare(first, base):
        def per_group(g, carry):
            at = pl.ds(pl.multiple_of(g * 8, 8), 8)
            component = me * rows + first + g * 8
            speed = wave_ref[component // ND]
            turn = pl.ds(pl.multiple_of(lax.rem(component, ND), 8), 8)
            own_x = trig_ref[0, turn, :] * speed
            own_y = trig_ref[1, turn, :] * speed
            taken = jnp.full((8, HALO), substeps_ref[component], jnp.int32)
            for i in range(1, 8):
                taken = jnp.where(sublane == i, substeps_ref[component + i], taken)
            count = taken.astype(jnp.float32)
            repeats[at] = count
            scale = courant_scale / count
            for i in range(1, window - 1):
                along_x = (own_x + currents[0, base + i]) * scale
                along_y = (own_y + currents[1, base + i]) * scale
                speeds[0, i, at] = jnp.clip(along_x, -courant_limit, courant_limit)
                speeds[1, i, at] = jnp.clip(along_y, -courant_limit, courant_limit)
            return carry

        lax.fori_loop(0, chunk // 8, per_group, 0)

    stacked = chunk % 16 == 0

    def pick(i, chosen):
        if stacked:
            pair = jnp.concatenate([parts[i], parts[i + 1]], axis=1)
            both = jnp.dot(pair, chosen, preferred_element_type=jnp.float32)
            taken = both[:chunk]
            for p in range(1, PARTS):
                taken = taken + both[p * chunk : (p + 1) * chunk]
        else:
            taken = None
            for p in range(PARTS):
                at = pl.ds(p * chunk, chunk)
                pair = jnp.concatenate([parts[i, at], parts[i + 1, at]], axis=1)
                term = jnp.dot(pair, chosen, preferred_element_type=jnp.float32)
                taken = term if taken is None else taken + term
        return taken[:, :HALO], taken[:, HALO:]

    def advance(first, b):
        base = b * block
        at = pl.ds(first, chunk)
        prepare(first, base)

        def state(s, i):
            if s == 0:
                return extended[at, pl.ds(pl.multiple_of((base + i) * HALO, HALO), HALO)]
            return states[s % 2, i]

        for s in range(SUB):
            for i in range(s, window - s):
                rest = state(s, i)
                for p in range(PARTS):
                    part = rest.astype(jnp.bfloat16)
                    parts[i, p * chunk : (p + 1) * chunk] = part
                    if p + 1 < PARTS:
                        rest = rest - part.astype(jnp.float32)
            for i in range(s + 1, window - 1 - s):
                value = state(s, i)
                west, south = pick(i - 1, selector[base + i, 0])
                east, north = pick(i, selector[base + i, 1])
                along_x = speeds[0, i]
                along_y = speeds[1, i]
                change = jnp.abs(along_x) * (value - jnp.where(along_x > 0.0, west, east))
                change = change + jnp.abs(along_y) * (
                    value - jnp.where(along_y > 0.0, south, north)
                )
                if s > 0:
                    change = jnp.where(repeats[...] > float(s), change, 0.0)
                if s + 1 < SUB:
                    states[(s + 1) % 2, i] = value - change
                else:
                    finals[base + i - SUB, at] = value - change

    def piece(k, first, count):
        target = lax.rem(me + k, peers)
        return remote(
            finals.at[target, pl.ds(first, count)],
            points_ref.at[pl.ds(pl.multiple_of(me * rows + first, 8), count)],
            piece_send.at[k],
            piece_recv.at[k],
            {"comp": target},
        )

    order = sorted(range(1, peers), key=lambda k: abs(k - peers / 2))
    load.wait()

    def step(c, carry):
        first = rows_of(c)
        to_left, to_right = halo(first, chunk, c)

        @pl.when(has_right)
        def _():
            to_left.wait_recv()

        @pl.when(has_left)
        def _():
            to_right.wait_recv()

        def per_block(b, inner):
            advance(first, b)
            return inner

        if tiles == block:
            advance(first, 0)
        else:
            lax.fori_loop(0, tiles // block, per_block, 0)

        @pl.when(goes_first)
        def _():
            for k in order:
                piece(k, first, chunk).start()

        return carry

    lax.fori_loop(0, chunks, step, 0)
    own = pltpu.make_async_copy(
        finals.at[me], points_ref.at[pl.ds(pl.multiple_of(me * rows, 8), rows)], own_sem
    )
    own.start()

    @pl.when(jnp.logical_not(goes_first))
    def _():
        pl.semaphore_wait(turn_sem, 1)
        for k in order:
            piece(k, 0, rows).start()

    for k in order:
        piece(k, 0, rows).wait_send()

    @pl.when(goes_first)
    def _():
        partner = here + 1 - 2 * odd
        pl.semaphore_signal(turn_sem, inc=1, device_id={"space": partner}, device_id_type=MESH)

    own.wait()
    to_left, to_right = halo(0, rows, 0)

    @pl.when(has_left)
    def _():
        to_left.wait_send()
        for copy in to_left_sides:
            copy.wait_send()

    @pl.when(has_right)
    def _():
        to_right.wait_send()
        for copy in to_right_sides:
            copy.wait_send()

    for k in order:
        piece(k, 0, rows).wait_recv()


def propagate(field, wave_speed, substeps, east, north, neighbours, peers, spaces):
    rows, width = field.shape
    tiles = width // HALO
    reach = SUB * HALO
    assert width >= reach and spaces % 2 == 0
    chunk = chunk_rows(rows)
    block = math.gcd(tiles, 4)
    outer = tiles + 2 * SUB
    window = block + 2 * SUB
    angles = (np.arange(ND, dtype=np.float32) + np.float32(0.5)) * np.float32(2.0 * math.pi / ND)
    trig = np.stack([np.cos(angles), np.sin(angles)])
    trig = np.ascontiguousarray(np.broadcast_to(trig[:, :, None], (2, ND, HALO)))
    vmem = pl.BlockSpec(memory_space=pltpu.VMEM)
    smem = pl.BlockSpec(memory_space=pltpu.SMEM)
    return pl.pallas_call(
        functools.partial(propagate_kernel, peers, spaces, chunk, block),
        out_shape=jax.ShapeDtypeStruct((peers * rows, HALO), jnp.float32),
        in_specs=[pl.BlockSpec(memory_space=pl.ANY), smem, smem, vmem, vmem, vmem, vmem],
        out_specs=vmem,
        scratch_shapes=[
            pltpu.VMEM((rows, width + 2 * reach), jnp.float32),
            pltpu.VMEM((tiles, rows, HALO), jnp.float32),
            pltpu.VMEM((2, 4, reach), jnp.int32),
            pltpu.VMEM((2, 2, 1, reach), jnp.float32),
            pltpu.VMEM((outer, 2, 2 * HALO, 2 * HALO), jnp.bfloat16),
            pltpu.VMEM((2, outer, 8, HALO), jnp.float32),
            pltpu.VMEM((2, window, chunk, HALO), jnp.float32),
            pltpu.VMEM((window, PARTS * chunk, HALO), jnp.bfloat16),
            pltpu.VMEM((2, window, chunk, HALO), jnp.float32),
            pltpu.VMEM((chunk, HALO), jnp.float32),
            pltpu.SemaphoreType.DMA,
            pltpu.SemaphoreType.DMA((2, 3)),
            pltpu.SemaphoreType.DMA((2, 3)),
            pltpu.SemaphoreType.DMA((2,)),
            pltpu.SemaphoreType.DMA((2, rows // chunk)),
            pltpu.SemaphoreType.DMA((peers,)),
            pltpu.SemaphoreType.DMA((peers,)),
            pltpu.SemaphoreType.DMA,
            pltpu.SemaphoreType.REGULAR,
        ],
        compiler_params=pltpu.CompilerParams(collective_id=0, has_side_effects=True),
    )(
        field,
        wave_speed,
        substeps,
        jnp.asarray(trig),
        east.reshape(1, width),
        north.reshape(1, width),
        neighbours,
    )


def source_kernel(batch, quad_ref, strength_ref, points_ref, blocks_ref, out_ref, rounded, products):
    total = blocks_ref.shape[0]

    def fill(f, carry):
        value = points_ref[f]
        rounded[f] = value.astype(jnp.bfloat16)
        out_ref[f] = value
        return carry

    lax.fori_loop(0, NF, fill, 0, unroll=4)

    def step(i, carry):
        for b in range(batch):
            j = i * batch + b
            block = blocks_ref[j]
            left = jnp.dot(block, rounded[quad_ref[0, j]], preferred_element_type=jnp.float32)
            right = lax.dot_general(
                block,
                rounded[quad_ref[1, j]],
                (((0,), (0,)), ((), ())),
                preferred_element_type=jnp.float32,
            )
            products[b] = (left * right * points_ref[quad_ref[2, j]]).astype(jnp.bfloat16)
        parts = []
        for b in range(batch):
            j = i * batch + b
            part = jnp.dot(blocks_ref[j], products[b], preferred_element_type=jnp.float32)
            parts.append(part * (strength_ref[j] * source_step))
        for b in range(batch):
            target = quad_ref[3, i * batch + b]
            out_ref[target] = out_ref[target] + parts[b]
        return carry

    lax.fori_loop(0, total // batch, step, 0)


def source_term(points, blocks, quad_index, strength):
    width = points.shape[1]
    vmem = pl.BlockSpec(memory_space=pltpu.VMEM)
    smem = pl.BlockSpec(memory_space=pltpu.SMEM)
    batch = math.gcd(blocks.shape[0], 32)
    out = pl.pallas_call(
        functools.partial(source_kernel, batch),
        out_shape=jax.ShapeDtypeStruct((NF, ND, width), jnp.float32),
        in_specs=[smem, smem, vmem, vmem],
        out_specs=vmem,
        scratch_shapes=[
            pltpu.VMEM((NF, ND, width), jnp.bfloat16),
            pltpu.VMEM((batch, ND, width), jnp.bfloat16),
        ],
    )(quad_index, strength, points.reshape(NF, ND, width), blocks)
    return out.reshape(NF * ND, width)


def home_kernel(peers, points_ref, out_ref, send_sem, recv_sem, own_sem):
    me = lax.axis_index("comp")
    rows = out_ref.shape[0]
    place = pl.ds(pl.multiple_of(me * HALO, HALO), HALO)
    own = pltpu.make_async_copy(
        points_ref.at[pl.ds(pl.multiple_of(me * rows, 8), rows)], out_ref.at[:, place], own_sem
    )
    own.start()
    sync(peers, 0)
    copies = []
    for k in sorted(range(1, peers), key=lambda k: abs(k - peers / 2)):
        target = lax.rem(me + k, peers)
        copy = pltpu.make_async_remote_copy(
            src_ref=points_ref.at[pl.ds(pl.multiple_of(target * rows, 8), rows)],
            dst_ref=out_ref.at[:, place],
            send_sem=send_sem.at[k],
            recv_sem=recv_sem.at[k],
            device_id={"comp": target},
            device_id_type=MESH,
        )
        copy.start()
        copies.append(copy)
    own.wait()
    for copy in copies:
        copy.wait()


def send_home(points, peers):
    rows = points.shape[0] // peers
    return pl.pallas_call(
        functools.partial(home_kernel, peers),
        out_shape=jax.ShapeDtypeStruct((rows, peers * HALO), jnp.float32),
        in_specs=[pl.BlockSpec(memory_space=pltpu.VMEM)],
        out_specs=pl.BlockSpec(memory_space=pltpu.VMEM),
        scratch_shapes=[
            pltpu.SemaphoreType.DMA((peers,)),
            pltpu.SemaphoreType.DMA((peers,)),
            pltpu.SemaphoreType.DMA,
        ],
        compiler_params=pltpu.CompilerParams(collective_id=1, has_side_effects=True),
    )(points)


def shards(
    spectrum,
    wave_speed,
    current_east,
    current_north,
    substeps,
    neighbours,
    blocks,
    quad_index,
    strength,
):
    peers = lax.axis_size("comp")
    spaces = lax.axis_size("space")
    rows, width = spectrum.shape
    assert width == peers * HALO
    points = propagate(
        spectrum, wave_speed, substeps, current_east, current_north, neighbours, peers, spaces
    )
    points = source_term(points, blocks, quad_index, strength)
    return send_home(points, peers)


def solution(mesh):
    in_specs = (
        P("comp", ("grp", "space")),
        P(),
        P(("grp", "space")),
        P(("grp", "space")),
        P(),
        P(None, ("grp", "space")),
        P(),
        P(),
        P(),
    )
    out_specs = P("comp", ("grp", "space"))
    return jax.shard_map(shards, mesh=mesh, in_specs=in_specs, out_specs=out_specs, check_vma=False)
```

```python
import functools
import math

import jax
import jax.numpy as jnp
import numpy as np
from jax import lax
from jax.experimental import pallas as pl
from jax.experimental.pallas import tpu as pltpu
from jax.sharding import PartitionSpec as P

NF = 36
ND = 64
SUB = 4
HALO = 128
PARTS = 2
EARLY = 0

courant_scale = 0.4
courant_limit = 0.45
source_step = 0.1

MESH = pl.DeviceIdType.MESH


def chunk_rows(rows):
    for size in (64, 72, 48, 32, 24, 16, 8):
        if rows % size == 0:
            return size
    return rows


def sync(peers, spaces):
    me = lax.axis_index("comp")
    here = lax.axis_index("space")
    barrier = pltpu.get_barrier_semaphore()
    count = 0
    for k in range(1, peers):
        pl.semaphore_signal(
            barrier, inc=1, device_id={"comp": lax.rem(me + k, peers)}, device_id_type=MESH
        )
        count += 1
    if spaces:
        for k in (1, spaces - 1):
            pl.semaphore_signal(
                barrier, inc=1, device_id={"space": lax.rem(here + k, spaces)}, device_id_type=MESH
            )
            count += 1
    pl.semaphore_wait(barrier, count)


def wave_kernel(
    peers,
    spaces,
    chunk,
    block,
    batch,
    early,
    field_ref,
    wave_ref,
    substeps_ref,
    trig_ref,
    east_ref,
    north_ref,
    neighbour_ref,
    quad_ref,
    strength_ref,
    blocks_ref,
    out_ref,
    points_ref,
    extended,
    finals,
    side_table,
    side_current,
    selector,
    currents,
    states,
    parts,
    speeds,
    repeats,
    links,
    chain,
    blocks,
    fields,
    rounded,
    products,
    slots,
    updated,
    load_sem,
    blocks_sem,
    chain_sem,
    side_send,
    side_recv,
    halo_send,
    halo_recv,
    piece_send,
    piece_recv,
    home_send,
    home_recv,
    own_sem,
    turn_sem,
):
    me = lax.axis_index("comp")
    here = lax.axis_index("space")
    rows, width = field_ref.shape
    tiles = width // HALO
    reach = SUB * HALO
    chunks = rows // chunk
    has_left = here > 0
    has_right = here < spaces - 1
    odd = lax.rem(here, 2)
    goes_first = odd == jnp.where(here < spaces // 2, 0, 1)

    load = pltpu.make_async_copy(field_ref, extended.at[:, pl.ds(reach, width)], load_sem)
    load.start()
    load_blocks = pltpu.make_async_copy(blocks_ref, blocks, blocks_sem)
    load_blocks.start()

    sync(peers, spaces)

    left = {"space": jnp.maximum(here - 1, 0)}
    right = {"space": jnp.minimum(here + 1, spaces - 1)}

    def remote(source, target, send, recv, device):
        return pltpu.make_async_remote_copy(
            src_ref=source,
            dst_ref=target,
            send_sem=send,
            recv_sem=recv,
            device_id=device,
            device_id_type=MESH,
        )

    def sides():
        copies = []
        for side, start, device in ((1, 0, left), (0, width - reach, right)):
            part = pl.ds(start, reach)
            pairs = (
                (neighbour_ref.at[:, part], side_table.at[side]),
                (east_ref.at[:, part], side_current.at[side, 0]),
                (north_ref.at[:, part], side_current.at[side, 1]),
            )
            copies.append(
                [
                    remote(source, target, side_send.at[side, i], side_recv.at[side, i], device)
                    for i, (source, target) in enumerate(pairs)
                ]
            )
        return copies

    def halo(first, count, sem):
        part = pl.ds(first, count)
        to_left = remote(
            field_ref.at[part, pl.ds(0, reach)],
            extended.at[part, pl.ds(reach + width, reach)],
            halo_send.at[1],
            halo_recv.at[1, sem],
            left,
        )
        to_right = remote(
            field_ref.at[part, pl.ds(width - reach, reach)],
            extended.at[part, pl.ds(0, reach)],
            halo_send.at[0],
            halo_recv.at[0, sem],
            right,
        )
        return to_left, to_right

    def rows_of(c):
        return pl.multiple_of(c * chunk, 8)

    to_left_sides, to_right_sides = sides()

    @pl.when(has_left)
    def _():
        for copy in to_left_sides:
            copy.start()

    @pl.when(has_right)
    def _():
        for copy in to_right_sides:
            copy.start()

    def start_halo(c, carry):
        to_left, to_right = halo(rows_of(c), chunk, c)

        @pl.when(has_left)
        def _():
            to_left.start()

        @pl.when(has_right)
        def _():
            to_right.start()

        return carry

    lax.fori_loop(0, chunks, start_halo, 0)

    lane = lax.broadcasted_iota(jnp.int32, (4, HALO), 1)
    for side, missing in ((0, jnp.logical_not(has_left)), (1, jnp.logical_not(has_right))):

        @pl.when(missing)
        def _(side=side):
            first = (tiles - SUB) * HALO if side == 0 else 0
            for i in range(SUB):
                part = pl.ds(i * HALO, HALO)
                side_table[side, :, part] = lane + (first + (i + 1) * HALO)
            side_current[side] = jnp.zeros((2, 1, reach), jnp.float32)
            start = 0 if side == 0 else reach + width

            def clear(g, carry):
                at = pl.ds(pl.multiple_of(g * 8, 8), 8)
                extended[at, pl.ds(start, reach)] = jnp.zeros((8, reach), jnp.float32)
                return carry

            lax.fori_loop(0, rows // 8, clear, 0)

    def spread(row):
        return jnp.broadcast_to(row, (8, HALO))

    spot = lax.broadcasted_iota(jnp.int32, (2 * HALO, HALO), 0)

    def fill(e, table_ref, east_row, north_row, tile, place):
        for d in range(4):
            wanted = table_ref[d : d + 1, place] - (tile + d % 2) * HALO
            half = d // 2 * HALO
            chosen = jnp.where(spot == wanted, 1.0, 0.0).astype(jnp.bfloat16)
            selector[e, d % 2, :, half : half + HALO] = chosen
        currents[0, e] = spread(east_row[:, place])
        currents[1, e] = spread(north_row[:, place])

    def fill_own(j, carry):
        fill(j + SUB, neighbour_ref, east_ref, north_ref, j, pl.ds(pl.multiple_of(j * HALO, HALO), HALO))
        return carry

    lax.fori_loop(0, tiles, fill_own, 0)

    total = blocks.shape[0]
    spots = lax.broadcasted_iota(jnp.int32, (1, HALO), 1)
    none = jnp.full((1, HALO), total, jnp.int32)

    def targets(j, row):
        return jnp.where(spots == j, quad_ref[3, j], row)

    def link(j, carry):
        before, last = carry
        target = quad_ref[3, j]
        before = jnp.where(jnp.logical_and(spots > j, row == target), j, before)
        last = jnp.where(spots == target, j, last)
        return before, last

    row = lax.fori_loop(0, total, targets, none)
    before, last = lax.fori_loop(0, total, link, (none, none))
    links[0:1] = before
    links[1:2] = last
    load_chain = pltpu.make_async_copy(links, chain, chain_sem)
    load_chain.start()
    slots[total] = jnp.zeros((ND, HALO), jnp.float32)

    @pl.when(has_right)
    def _():
        for copy in to_left_sides:
            copy.wait_recv()

    @pl.when(has_left)
    def _():
        for copy in to_right_sides:
            copy.wait_recv()

    for i in range(SUB):
        place = pl.ds(i * HALO, HALO)
        fill(i, side_table.at[0], side_current.at[0, 0], side_current.at[0, 1], tiles - SUB + i, place)
        fill(
            SUB + tiles + i, side_table.at[1], side_current.at[1, 0], side_current.at[1, 1], i, place
        )

    sublane = lax.broadcasted_iota(jnp.int32, (8, HALO), 0)
    window = block + 2 * SUB

    def prepare(first, base):
        def per_group(g, carry):
            at = pl.ds(pl.multiple_of(g * 8, 8), 8)
            component = me * rows + first + g * 8
            speed = wave_ref[component // ND]
            turn = pl.ds(pl.multiple_of(lax.rem(component, ND), 8), 8)
            own_x = trig_ref[0, turn, :] * speed
            own_y = trig_ref[1, turn, :] * speed
            taken = jnp.full((8, HALO), substeps_ref[component], jnp.int32)
            for i in range(1, 8):
                taken = jnp.where(sublane == i, substeps_ref[component + i], taken)
            count = taken.astype(jnp.float32)
            repeats[at] = count
            scale = courant_scale / count
            for i in range(1, window - 1):
                along_x = (own_x + currents[0, base + i]) * scale
                along_y = (own_y + currents[1, base + i]) * scale
                speeds[0, i, at] = jnp.clip(along_x, -courant_limit, courant_limit)
                speeds[1, i, at] = jnp.clip(along_y, -courant_limit, courant_limit)
            return carry

        lax.fori_loop(0, chunk // 8, per_group, 0)

    stacked = chunk % 16 == 0

    def pick(i, chosen):
        if stacked:
            pair = jnp.concatenate([parts[i], parts[i + 1]], axis=1)
            both = jnp.dot(pair, chosen, preferred_element_type=jnp.float32)
            taken = both[:chunk]
            for p in range(1, PARTS):
                taken = taken + both[p * chunk : (p + 1) * chunk]
        else:
            taken = None
            for p in range(PARTS):
                at = pl.ds(p * chunk, chunk)
                pair = jnp.concatenate([parts[i, at], parts[i + 1, at]], axis=1)
                term = jnp.dot(pair, chosen, preferred_element_type=jnp.float32)
                taken = term if taken is None else taken + term
        return taken[:, :HALO], taken[:, HALO:]

    def advance(first, b):
        base = b * block
        at = pl.ds(first, chunk)
        prepare(first, base)

        def state(s, i):
            if s == 0:
                return extended[at, pl.ds(pl.multiple_of((base + i) * HALO, HALO), HALO)]
            return states[s % 2, i]

        for s in range(SUB):
            for i in range(s, window - s):
                rest = state(s, i)
                for p in range(PARTS):
                    part = rest.astype(jnp.bfloat16)
                    parts[i, p * chunk : (p + 1) * chunk] = part
                    if p + 1 < PARTS:
                        rest = rest - part.astype(jnp.float32)
            for i in range(s + 1, window - 1 - s):
                value = state(s, i)
                west, south = pick(i - 1, selector[base + i, 0])
                east, north = pick(i, selector[base + i, 1])
                along_x = speeds[0, i]
                along_y = speeds[1, i]
                change = jnp.abs(along_x) * (value - jnp.where(along_x > 0.0, west, east))
                change = change + jnp.abs(along_y) * (
                    value - jnp.where(along_y > 0.0, south, north)
                )
                if s > 0:
                    change = jnp.where(repeats[...] > float(s), change, 0.0)
                if s + 1 < SUB:
                    states[(s + 1) % 2, i] = value - change
                else:
                    finals[base + i - SUB, at] = value - change

    def piece(k, first, count):
        target = lax.rem(me + k, peers)
        return remote(
            finals.at[target, pl.ds(first, count)],
            points_ref.at[pl.ds(pl.multiple_of(me * rows + first, 8), count)],
            piece_send.at[k],
            piece_recv.at[k],
            {"comp": target},
        )

    order = sorted(range(1, peers), key=lambda k: abs(k - peers / 2))
    load.wait()

    def step(c, carry):
        first = rows_of(c)
        to_left, to_right = halo(first, chunk, c)

        @pl.when(has_right)
        def _():
            to_left.wait_recv()

        @pl.when(has_left)
        def _():
            to_right.wait_recv()

        def per_block(b, inner):
            advance(first, b)
            return inner

        if tiles == block:
            advance(first, 0)
        else:
            lax.fori_loop(0, tiles // block, per_block, 0)

        @pl.when(jnp.logical_or(goes_first, c < early))
        def _():
            for k in order:
                piece(k, first, chunk).start()

        return carry

    lax.fori_loop(0, chunks, step, 0)
    place = pl.ds(pl.multiple_of(me * rows, 8), rows)
    own = pltpu.make_async_copy(finals.at[me], points_ref.at[place], own_sem)
    own.start()

    @pl.when(jnp.logical_not(goes_first))
    def _():
        pl.semaphore_wait(turn_sem.at[0], 1)
        if early < chunks:
            for k in order:
                piece(k, early * chunk, rows - early * chunk).start()

    for k in order:
        piece(k, 0, rows).wait_send()
    partner = {"space": here + 1 - 2 * odd}

    @pl.when(goes_first)
    def _():
        pl.semaphore_signal(turn_sem.at[0], inc=1, device_id=partner, device_id_type=MESH)

    @pl.when(jnp.logical_not(goes_first))
    def _():
        pl.semaphore_signal(turn_sem.at[1], inc=1, device_id=partner, device_id_type=MESH)

    own.wait()
    load_blocks.wait()
    load_chain.wait()
    for k in order:
        piece(k, 0, rows).wait_recv()

    def frequency(f):
        return pl.ds(pl.multiple_of(f * ND, ND), ND)

    def take(f, carry):
        value = points_ref[frequency(f)]
        rounded[f] = value.astype(jnp.bfloat16)
        fields[f] = value
        return carry

    lax.fori_loop(0, NF, take, 0, unroll=4)

    def interact(i, carry):
        for b in range(batch):
            j = i * batch + b
            matrix = blocks[j]
            left_term = jnp.dot(matrix, rounded[quad_ref[0, j]], preferred_element_type=jnp.float32)
            right_term = lax.dot_general(
                matrix,
                rounded[quad_ref[1, j]],
                (((0,), (0,)), ((), ())),
                preferred_element_type=jnp.float32,
            )
            products[b] = (left_term * right_term * fields[quad_ref[2, j]]).astype(jnp.bfloat16)
        terms = []
        for b in range(batch):
            j = i * batch + b
            term = jnp.dot(blocks[j], products[b], preferred_element_type=jnp.float32)
            terms.append(term * (strength_ref[j] * source_step))
        for b in range(batch):
            j = i * batch + b
            slots[j] = slots[chain[0, j]] + terms[b]
        return carry

    lax.fori_loop(0, total // batch, interact, 0)

    def finish(f, carry):
        updated[frequency(f)] = fields[f] + slots[chain[1, f]]
        return carry

    lax.fori_loop(0, NF, finish, 0, unroll=4)

    @pl.when(goes_first)
    def _():
        pl.semaphore_wait(turn_sem.at[1], 1)

    column = pl.ds(pl.multiple_of(me * HALO, HALO), HALO)
    homes = []
    for k in order:
        target = lax.rem(me + k, peers)
        home = remote(
            updated.at[pl.ds(pl.multiple_of(target * rows, 8), rows)],
            out_ref.at[:, column],
            home_send.at[k],
            home_recv.at[k],
            {"comp": target},
        )
        home.start()
        homes.append(home)
    own = pltpu.make_async_copy(updated.at[place], out_ref.at[:, column], own_sem)
    own.start()
    to_left, to_right = halo(0, rows, 0)

    @pl.when(has_left)
    def _():
        to_left.wait_send()
        for copy in to_left_sides:
            copy.wait_send()

    @pl.when(has_right)
    def _():
        to_right.wait_send()
        for copy in to_right_sides:
            copy.wait_send()

    own.wait()
    for home in homes:
        home.wait()


def advance_waves(
    field, wave_speed, substeps, east, north, neighbours, blocks, quad_index, strength, peers, spaces
):
    rows, width = field.shape
    tiles = width // HALO
    reach = SUB * HALO
    total = blocks.shape[0]
    assert width >= reach and spaces % 2 == 0 and max(total, NF) < HALO
    chunk = chunk_rows(rows)
    block = math.gcd(tiles, 4)
    outer = tiles + 2 * SUB
    window = block + 2 * SUB
    batch = math.gcd(total, 32)
    early = min(EARLY, rows // chunk)
    angles = (np.arange(ND, dtype=np.float32) + np.float32(0.5)) * np.float32(2.0 * math.pi / ND)
    trig = np.stack([np.cos(angles), np.sin(angles)])
    trig = np.ascontiguousarray(np.broadcast_to(trig[:, :, None], (2, ND, HALO)))
    vmem = pl.BlockSpec(memory_space=pltpu.VMEM)
    smem = pl.BlockSpec(memory_space=pltpu.SMEM)
    whole = pl.BlockSpec(memory_space=pl.ANY)
    return pl.pallas_call(
        functools.partial(wave_kernel, peers, spaces, chunk, block, batch, early),
        out_shape=jax.ShapeDtypeStruct((rows, width), jnp.float32),
        in_specs=[whole, smem, smem, vmem, vmem, vmem, vmem, smem, smem, whole],
        out_specs=whole,
        scratch_shapes=[
            pltpu.VMEM((peers * rows, HALO), jnp.float32),
            pltpu.VMEM((rows, width + 2 * reach), jnp.float32),
            pltpu.VMEM((tiles, rows, HALO), jnp.float32),
            pltpu.VMEM((2, 4, reach), jnp.int32),
            pltpu.VMEM((2, 2, 1, reach), jnp.float32),
            pltpu.VMEM((outer, 2, 2 * HALO, 2 * HALO), jnp.bfloat16),
            pltpu.VMEM((2, outer, 8, HALO), jnp.float32),
            pltpu.VMEM((2, window, chunk, HALO), jnp.float32),
            pltpu.VMEM((window, PARTS * chunk, HALO), jnp.bfloat16),
            pltpu.VMEM((2, window, chunk, HALO), jnp.float32),
            pltpu.VMEM((chunk, HALO), jnp.float32),
            pltpu.VMEM((8, HALO), jnp.int32),
            pltpu.SMEM((8, HALO), jnp.int32),
            pltpu.VMEM(blocks.shape, jnp.bfloat16),
            pltpu.VMEM((NF, ND, HALO), jnp.float32),
            pltpu.VMEM((NF, ND, HALO), jnp.bfloat16),
            pltpu.VMEM((batch, ND, HALO), jnp.bfloat16),
            pltpu.VMEM((total + 1, ND, HALO), jnp.float32),
            pltpu.VMEM((peers * rows, HALO), jnp.float32),
            pltpu.SemaphoreType.DMA,
            pltpu.SemaphoreType.DMA,
            pltpu.SemaphoreType.DMA,
            pltpu.SemaphoreType.DMA((2, 3)),
            pltpu.SemaphoreType.DMA((2, 3)),
            pltpu.SemaphoreType.DMA((2,)),
            pltpu.SemaphoreType.DMA((2, rows // chunk)),
            pltpu.SemaphoreType.DMA((peers,)),
            pltpu.SemaphoreType.DMA((peers,)),
            pltpu.SemaphoreType.DMA((peers,)),
            pltpu.SemaphoreType.DMA((peers,)),
            pltpu.SemaphoreType.DMA,
            pltpu.SemaphoreType.REGULAR((2,)),
        ],
        compiler_params=pltpu.CompilerParams(collective_id=0, has_side_effects=True),
    )(
        field,
        wave_speed,
        substeps,
        jnp.asarray(trig),
        east.reshape(1, width),
        north.reshape(1, width),
        neighbours,
        quad_index,
        strength,
        blocks,
    )


def shards(
    spectrum,
    wave_speed,
    current_east,
    current_north,
    substeps,
    neighbours,
    blocks,
    quad_index,
    strength,
):
    peers = lax.axis_size("comp")
    spaces = lax.axis_size("space")
    rows, width = spectrum.shape
    assert width == peers * HALO
    return advance_waves(
        spectrum,
        wave_speed,
        substeps,
        current_east,
        current_north,
        neighbours,
        blocks,
        quad_index,
        strength,
        peers,
        spaces,
    )


def solution(mesh):
    in_specs = (
        P("comp", ("grp", "space")),
        P(),
        P(("grp", "space")),
        P(("grp", "space")),
        P(),
        P(None, ("grp", "space")),
        P(),
        P(),
        P(),
    )
    out_specs = P("comp", ("grp", "space"))
    return jax.shard_map(shards, mesh=mesh, in_specs=in_specs, out_specs=out_specs, check_vma=False)
```

```python
import functools
import math

import jax
import jax.numpy as jnp
import numpy as np
from jax import lax
from jax.experimental import pallas as pl
from jax.experimental.pallas import tpu as pltpu
from jax.sharding import PartitionSpec as P

NF = 36
ND = 64
SUB = 4
HALO = 128
PARTS = 2
EARLY = 2
LATE = 2

courant_scale = 0.4
courant_limit = 0.45
source_step = 0.1

MESH = pl.DeviceIdType.MESH


def chunk_rows(rows):
    for size in (64, 72, 48, 32, 24, 16, 8):
        if rows % size == 0:
            return size
    return rows


def greet(peers, spaces):
    me = lax.axis_index("comp")
    here = lax.axis_index("space")
    barrier = pltpu.get_barrier_semaphore()
    count = 0
    for k in range(1, peers):
        pl.semaphore_signal(
            barrier, inc=1, device_id={"comp": lax.rem(me + k, peers)}, device_id_type=MESH
        )
        count += 1
    for k in (1, spaces - 1):
        pl.semaphore_signal(
            barrier, inc=1, device_id={"space": lax.rem(here + k, spaces)}, device_id_type=MESH
        )
        count += 1
    return barrier, count


def wave_kernel(
    peers,
    spaces,
    chunk,
    block,
    batch,
    early,
    late,
    field_ref,
    wave_ref,
    substeps_ref,
    trig_ref,
    east_ref,
    north_ref,
    neighbour_ref,
    quad_ref,
    strength_ref,
    blocks_ref,
    out_ref,
    points_ref,
    extended,
    finals,
    side_table,
    side_current,
    selector,
    currents,
    states,
    parts,
    speeds,
    repeats,
    links,
    chain,
    blocks,
    fields,
    rounded,
    products,
    slots,
    updated,
    load_sem,
    blocks_sem,
    chain_sem,
    side_send,
    side_recv,
    halo_send,
    halo_recv,
    piece_send,
    piece_recv,
    home_send,
    home_recv,
    own_sem,
    turn_sem,
):
    me = lax.axis_index("comp")
    here = lax.axis_index("space")
    rows, width = field_ref.shape
    tiles = width // HALO
    reach = SUB * HALO
    chunks = rows // chunk
    has_left = here > 0
    has_right = here < spaces - 1
    odd = lax.rem(here, 2)
    goes_first = odd == jnp.where(here < spaces // 2, 0, 1)

    load = pltpu.make_async_copy(field_ref, extended.at[:, pl.ds(reach, width)], load_sem)
    load.start()
    load_blocks = pltpu.make_async_copy(blocks_ref, blocks, blocks_sem)
    load_blocks.start()

    barrier, greetings = greet(peers, spaces)
    lane = lax.broadcasted_iota(jnp.int32, (4, HALO), 1)
    for side, missing in ((0, jnp.logical_not(has_left)), (1, jnp.logical_not(has_right))):

        @pl.when(missing)
        def _(side=side):
            first = (tiles - SUB) * HALO if side == 0 else 0
            for i in range(SUB):
                part = pl.ds(i * HALO, HALO)
                side_table[side, :, part] = lane + (first + (i + 1) * HALO)
            side_current[side] = jnp.zeros((2, 1, reach), jnp.float32)
            start = 0 if side == 0 else reach + width

            def clear(g, carry):
                at = pl.ds(pl.multiple_of(g * 8, 8), 8)
                extended[at, pl.ds(start, reach)] = jnp.zeros((8, reach), jnp.float32)
                return carry

            lax.fori_loop(0, rows // 8, clear, 0)

    def spread(row):
        return jnp.broadcast_to(row, (8, HALO))

    spot = lax.broadcasted_iota(jnp.int32, (2 * HALO, HALO), 0)

    def fill(e, table_ref, east_row, north_row, tile, place):
        for d in range(4):
            wanted = table_ref[d : d + 1, place] - (tile + d % 2) * HALO
            half = d // 2 * HALO
            chosen = jnp.where(spot == wanted, 1.0, 0.0).astype(jnp.bfloat16)
            selector[e, d % 2, :, half : half + HALO] = chosen
        currents[0, e] = spread(east_row[:, place])
        currents[1, e] = spread(north_row[:, place])

    def fill_own(j, carry):
        fill(j + SUB, neighbour_ref, east_ref, north_ref, j, pl.ds(pl.multiple_of(j * HALO, HALO), HALO))
        return carry

    lax.fori_loop(0, tiles, fill_own, 0)

    total = blocks.shape[0]
    spots = lax.broadcasted_iota(jnp.int32, (1, HALO), 1)
    none = jnp.full((1, HALO), total, jnp.int32)

    def targets(j, row):
        return jnp.where(spots == j, quad_ref[3, j], row)

    def link(j, carry):
        before, last = carry
        target = quad_ref[3, j]
        before = jnp.where(jnp.logical_and(spots > j, row == target), j, before)
        last = jnp.where(spots == target, j, last)
        return before, last

    row = lax.fori_loop(0, total, targets, none)
    before, last = lax.fori_loop(0, total, link, (none, none))
    links[0:1] = before
    links[1:2] = last
    load_chain = pltpu.make_async_copy(links, chain, chain_sem)
    load_chain.start()
    slots[total] = jnp.zeros((ND, HALO), jnp.float32)

    pl.semaphore_wait(barrier, greetings)

    left = {"space": jnp.maximum(here - 1, 0)}
    right = {"space": jnp.minimum(here + 1, spaces - 1)}

    def remote(source, target, send, recv, device):
        return pltpu.make_async_remote_copy(
            src_ref=source,
            dst_ref=target,
            send_sem=send,
            recv_sem=recv,
            device_id=device,
            device_id_type=MESH,
        )

    def sides():
        copies = []
        for side, start, device in ((1, 0, left), (0, width - reach, right)):
            part = pl.ds(start, reach)
            pairs = (
                (neighbour_ref.at[:, part], side_table.at[side]),
                (east_ref.at[:, part], side_current.at[side, 0]),
                (north_ref.at[:, part], side_current.at[side, 1]),
            )
            copies.append(
                [
                    remote(source, target, side_send.at[side, i], side_recv.at[side, i], device)
                    for i, (source, target) in enumerate(pairs)
                ]
            )
        return copies

    def halo(first, count, sem):
        part = pl.ds(first, count)
        to_left = remote(
            field_ref.at[part, pl.ds(0, reach)],
            extended.at[part, pl.ds(reach + width, reach)],
            halo_send.at[1],
            halo_recv.at[1, sem],
            left,
        )
        to_right = remote(
            field_ref.at[part, pl.ds(width - reach, reach)],
            extended.at[part, pl.ds(0, reach)],
            halo_send.at[0],
            halo_recv.at[0, sem],
            right,
        )
        return to_left, to_right

    def rows_of(c):
        return pl.multiple_of(c * chunk, 8)

    to_left_sides, to_right_sides = sides()

    @pl.when(has_left)
    def _():
        for copy in to_left_sides:
            copy.start()

    @pl.when(has_right)
    def _():
        for copy in to_right_sides:
            copy.start()

    def start_halo(c, carry):
        to_left, to_right = halo(rows_of(c), chunk, c)

        @pl.when(has_left)
        def _():
            to_left.start()

        @pl.when(has_right)
        def _():
            to_right.start()

        return carry

    lax.fori_loop(0, chunks, start_halo, 0)

    @pl.when(has_right)
    def _():
        for copy in to_left_sides:
            copy.wait_recv()

    @pl.when(has_left)
    def _():
        for copy in to_right_sides:
            copy.wait_recv()

    for i in range(SUB):
        place = pl.ds(i * HALO, HALO)
        fill(i, side_table.at[0], side_current.at[0, 0], side_current.at[0, 1], tiles - SUB + i, place)
        fill(
            SUB + tiles + i, side_table.at[1], side_current.at[1, 0], side_current.at[1, 1], i, place
        )

    sublane = lax.broadcasted_iota(jnp.int32, (8, HALO), 0)
    window = block + 2 * SUB

    def prepare(first, base):
        def per_group(g, carry):
            at = pl.ds(pl.multiple_of(g * 8, 8), 8)
            component = me * rows + first + g * 8
            speed = wave_ref[component // ND]
            turn = pl.ds(pl.multiple_of(lax.rem(component, ND), 8), 8)
            own_x = trig_ref[0, turn, :] * speed
            own_y = trig_ref[1, turn, :] * speed
            taken = jnp.full((8, HALO), substeps_ref[component], jnp.int32)
            for i in range(1, 8):
                taken = jnp.where(sublane == i, substeps_ref[component + i], taken)
            count = taken.astype(jnp.float32)
            repeats[at] = count
            scale = courant_scale / count
            for i in range(1, window - 1):
                along_x = (own_x + currents[0, base + i]) * scale
                along_y = (own_y + currents[1, base + i]) * scale
                speeds[0, i, at] = jnp.clip(along_x, -courant_limit, courant_limit)
                speeds[1, i, at] = jnp.clip(along_y, -courant_limit, courant_limit)
            return carry

        lax.fori_loop(0, chunk // 8, per_group, 0)

    stacked = chunk % 16 == 0

    def pick(i, chosen):
        if stacked:
            pair = jnp.concatenate([parts[i], parts[i + 1]], axis=1)
            both = jnp.dot(pair, chosen, preferred_element_type=jnp.float32)
            taken = both[:chunk]
            for p in range(1, PARTS):
                taken = taken + both[p * chunk : (p + 1) * chunk]
        else:
            taken = None
            for p in range(PARTS):
                at = pl.ds(p * chunk, chunk)
                pair = jnp.concatenate([parts[i, at], parts[i + 1, at]], axis=1)
                term = jnp.dot(pair, chosen, preferred_element_type=jnp.float32)
                taken = term if taken is None else taken + term
        return taken[:, :HALO], taken[:, HALO:]

    def advance(first, b):
        base = b * block
        at = pl.ds(first, chunk)
        prepare(first, base)

        def state(s, i):
            if s == 0:
                return extended[at, pl.ds(pl.multiple_of((base + i) * HALO, HALO), HALO)]
            return states[s % 2, i]

        for s in range(SUB):
            for i in range(s, window - s):
                rest = state(s, i)
                for p in range(PARTS):
                    part = rest.astype(jnp.bfloat16)
                    parts[i, p * chunk : (p + 1) * chunk] = part
                    if p + 1 < PARTS:
                        rest = rest - part.astype(jnp.float32)
            for i in range(s + 1, window - 1 - s):
                value = state(s, i)
                west, south = pick(i - 1, selector[base + i, 0])
                east, north = pick(i, selector[base + i, 1])
                along_x = speeds[0, i]
                along_y = speeds[1, i]
                change = jnp.abs(along_x) * (value - jnp.where(along_x > 0.0, west, east))
                change = change + jnp.abs(along_y) * (
                    value - jnp.where(along_y > 0.0, south, north)
                )
                if s > 0:
                    change = jnp.where(repeats[...] > float(s), change, 0.0)
                if s + 1 < SUB:
                    states[(s + 1) % 2, i] = value - change
                else:
                    finals[base + i - SUB, at] = value - change

    def piece(k, first, count, group):
        target = lax.rem(me + k, peers)
        return remote(
            finals.at[target, pl.ds(first, count)],
            points_ref.at[pl.ds(pl.multiple_of(me * rows + first, 8), count)],
            piece_send.at[group, k],
            piece_recv.at[k],
            {"comp": target},
        )

    order = sorted(range(1, peers), key=lambda k: abs(k - peers / 2))
    load.wait()

    def step(c, carry):
        first = rows_of(c)
        to_left, to_right = halo(first, chunk, c)

        @pl.when(has_right)
        def _():
            to_left.wait_recv()

        @pl.when(has_left)
        def _():
            to_right.wait_recv()

        def per_block(b, inner):
            advance(first, b)
            return inner

        if tiles == block:
            advance(first, 0)
        else:
            lax.fori_loop(0, tiles // block, per_block, 0)

        @pl.when(jnp.logical_or(goes_first, c < early))
        def _():
            for k in order:
                piece(k, first, chunk, jnp.where(c < chunks - late, 0, 1)).start()

        return carry

    lax.fori_loop(0, chunks, step, 0)
    place = pl.ds(pl.multiple_of(me * rows, 8), rows)
    own = pltpu.make_async_copy(finals.at[me], points_ref.at[place], own_sem)
    own.start()
    most = (chunks - late) * chunk

    @pl.when(jnp.logical_not(goes_first))
    def _():
        pl.semaphore_wait(turn_sem.at[0], 1)
        if early < chunks - late:
            for k in order:
                piece(k, early * chunk, most - early * chunk, 0).start()
        if late:
            for k in order:
                piece(k, most, rows - most, 1).start()

    for k in order:
        piece(k, 0, most, 0).wait_send()
    partner = {"space": here + 1 - 2 * odd}

    @pl.when(goes_first)
    def _():
        pl.semaphore_signal(turn_sem.at[0], inc=1, device_id=partner, device_id_type=MESH)

    @pl.when(jnp.logical_not(goes_first))
    def _():
        pl.semaphore_signal(turn_sem.at[1], inc=1, device_id=partner, device_id_type=MESH)

    own.wait()
    load_blocks.wait()
    load_chain.wait()
    for k in order:
        piece(k, 0, rows, 0).wait_recv()

    def frequency(f):
        return pl.ds(pl.multiple_of(f * ND, ND), ND)

    def take(f, carry):
        value = points_ref[frequency(f)]
        rounded[f] = value.astype(jnp.bfloat16)
        fields[f] = value
        return carry

    lax.fori_loop(0, NF, take, 0, unroll=4)

    def interact(i, carry):
        for b in range(batch):
            j = i * batch + b
            matrix = blocks[j]
            left_term = jnp.dot(matrix, rounded[quad_ref[0, j]], preferred_element_type=jnp.float32)
            right_term = lax.dot_general(
                matrix,
                rounded[quad_ref[1, j]],
                (((0,), (0,)), ((), ())),
                preferred_element_type=jnp.float32,
            )
            products[b] = (left_term * right_term * fields[quad_ref[2, j]]).astype(jnp.bfloat16)
        terms = []
        for b in range(batch):
            j = i * batch + b
            term = jnp.dot(blocks[j], products[b], preferred_element_type=jnp.float32)
            terms.append(term * (strength_ref[j] * source_step))
        for b in range(batch):
            j = i * batch + b
            slots[j] = slots[chain[0, j]] + terms[b]
        return carry

    lax.fori_loop(0, total // batch, interact, 0)

    def finish(f, carry):
        updated[frequency(f)] = fields[f] + slots[chain[1, f]]
        return carry

    lax.fori_loop(0, NF, finish, 0, unroll=4)

    @pl.when(goes_first)
    def _():
        pl.semaphore_wait(turn_sem.at[1], 1)

    column = pl.ds(pl.multiple_of(me * HALO, HALO), HALO)
    homes = []
    for k in order:
        target = lax.rem(me + k, peers)
        home = remote(
            updated.at[pl.ds(pl.multiple_of(target * rows, 8), rows)],
            out_ref.at[:, column],
            home_send.at[k],
            home_recv.at[k],
            {"comp": target},
        )
        home.start()
        homes.append(home)
    own = pltpu.make_async_copy(updated.at[place], out_ref.at[:, column], own_sem)
    own.start()
    to_left, to_right = halo(0, rows, 0)

    @pl.when(has_left)
    def _():
        to_left.wait_send()
        for copy in to_left_sides:
            copy.wait_send()

    @pl.when(has_right)
    def _():
        to_right.wait_send()
        for copy in to_right_sides:
            copy.wait_send()

    own.wait()
    if late:
        for k in order:
            piece(k, most, rows - most, 1).wait_send()
    for home in homes:
        home.wait()


def advance_waves(
    field, wave_speed, substeps, east, north, neighbours, blocks, quad_index, strength, peers, spaces
):
    rows, width = field.shape
    tiles = width // HALO
    reach = SUB * HALO
    total = blocks.shape[0]
    assert width >= reach and spaces % 2 == 0 and max(total, NF) < HALO
    chunk = chunk_rows(rows)
    block = math.gcd(tiles, 4)
    outer = tiles + 2 * SUB
    window = block + 2 * SUB
    batch = math.gcd(total, 32)
    late = min(LATE, rows // chunk - 1)
    early = min(EARLY, rows // chunk - late)
    angles = (np.arange(ND, dtype=np.float32) + np.float32(0.5)) * np.float32(2.0 * math.pi / ND)
    trig = np.stack([np.cos(angles), np.sin(angles)])
    trig = np.ascontiguousarray(np.broadcast_to(trig[:, :, None], (2, ND, HALO)))
    vmem = pl.BlockSpec(memory_space=pltpu.VMEM)
    smem = pl.BlockSpec(memory_space=pltpu.SMEM)
    whole = pl.BlockSpec(memory_space=pl.ANY)
    return pl.pallas_call(
        functools.partial(wave_kernel, peers, spaces, chunk, block, batch, early, late),
        out_shape=pltpu.VMEM((rows, width), jnp.float32),
        in_specs=[whole, smem, smem, vmem, vmem, vmem, vmem, smem, smem, whole],
        out_specs=vmem,
        scratch_shapes=[
            pltpu.VMEM((peers * rows, HALO), jnp.float32),
            pltpu.VMEM((rows, width + 2 * reach), jnp.float32),
            pltpu.VMEM((tiles, rows, HALO), jnp.float32),
            pltpu.VMEM((2, 4, reach), jnp.int32),
            pltpu.VMEM((2, 2, 1, reach), jnp.float32),
            pltpu.VMEM((outer, 2, 2 * HALO, 2 * HALO), jnp.bfloat16),
            pltpu.VMEM((2, outer, 8, HALO), jnp.float32),
            pltpu.VMEM((2, window, chunk, HALO), jnp.float32),
            pltpu.VMEM((window, PARTS * chunk, HALO), jnp.bfloat16),
            pltpu.VMEM((2, window, chunk, HALO), jnp.float32),
            pltpu.VMEM((chunk, HALO), jnp.float32),
            pltpu.VMEM((8, HALO), jnp.int32),
            pltpu.SMEM((8, HALO), jnp.int32),
            pltpu.VMEM(blocks.shape, jnp.bfloat16),
            pltpu.VMEM((NF, ND, HALO), jnp.float32),
            pltpu.VMEM((NF, ND, HALO), jnp.bfloat16),
            pltpu.VMEM((batch, ND, HALO), jnp.bfloat16),
            pltpu.VMEM((total + 1, ND, HALO), jnp.float32),
            pltpu.VMEM((peers * rows, HALO), jnp.float32),
            pltpu.SemaphoreType.DMA,
            pltpu.SemaphoreType.DMA,
            pltpu.SemaphoreType.DMA,
            pltpu.SemaphoreType.DMA((2, 3)),
            pltpu.SemaphoreType.DMA((2, 3)),
            pltpu.SemaphoreType.DMA((2,)),
            pltpu.SemaphoreType.DMA((2, rows // chunk)),
            pltpu.SemaphoreType.DMA((2, peers)),
            pltpu.SemaphoreType.DMA((peers,)),
            pltpu.SemaphoreType.DMA((peers,)),
            pltpu.SemaphoreType.DMA((peers,)),
            pltpu.SemaphoreType.DMA,
            pltpu.SemaphoreType.REGULAR((2,)),
        ],
        compiler_params=pltpu.CompilerParams(collective_id=0, has_side_effects=True),
    )(
        field,
        wave_speed,
        substeps,
        jnp.asarray(trig),
        east.reshape(1, width),
        north.reshape(1, width),
        neighbours,
        quad_index,
        strength,
        blocks,
    )


def shards(
    spectrum,
    wave_speed,
    current_east,
    current_north,
    substeps,
    neighbours,
    blocks,
    quad_index,
    strength,
):
    peers = lax.axis_size("comp")
    spaces = lax.axis_size("space")
    rows, width = spectrum.shape
    assert width == peers * HALO
    return advance_waves(
        spectrum,
        wave_speed,
        substeps,
        current_east,
        current_north,
        neighbours,
        blocks,
        quad_index,
        strength,
        peers,
        spaces,
    )


def solution(mesh):
    in_specs = (
        P("comp", ("grp", "space")),
        P(),
        P(("grp", "space")),
        P(("grp", "space")),
        P(),
        P(None, ("grp", "space")),
        P(),
        P(),
        P(),
    )
    out_specs = P("comp", ("grp", "space"))
    return jax.shard_map(shards, mesh=mesh, in_specs=in_specs, out_specs=out_specs, check_vma=False)
```

```python
import functools
import math

import jax
import jax.numpy as jnp
import numpy as np
from jax import lax
from jax.experimental import pallas as pl
from jax.experimental.pallas import tpu as pltpu
from jax.sharding import PartitionSpec as P

NF = 36
ND = 64
SUB = 4
HALO = 128
PARTS = 2
EARLY = 2
LATE_FIRST = 2
LATE_SECOND = 4

courant_scale = 0.4
courant_limit = 0.45
source_step = 0.1

MESH = pl.DeviceIdType.MESH


def chunk_rows(rows):
    for size in (64, 72, 48, 32, 24, 16, 8):
        if rows % size == 0:
            return size
    return rows


def greet(peers, spaces):
    me = lax.axis_index("comp")
    here = lax.axis_index("space")
    barrier = pltpu.get_barrier_semaphore()
    count = 0
    for axis, place, size in (("comp", me, peers), ("space", here, spaces)):
        for step, near in ((-1, place > 0), (1, place < size - 1)):

            @pl.when(near)
            def _(axis=axis, place=place, step=step):
                pl.semaphore_signal(
                    barrier, inc=1, device_id={axis: place + step}, device_id_type=MESH
                )

            count = count + jnp.where(near, 1, 0)
    return barrier, count


def pass_word(peers, word_sem):
    me = lax.axis_index("comp")

    def onward(side, waits, step):
        @pl.when(waits)
        def _():
            pl.semaphore_wait(word_sem.at[side], 1)

        pl.semaphore_signal(
            word_sem.at[side], inc=1, device_id={"comp": me + step}, device_id_type=MESH
        )

    def up():
        onward(0, me > 1, 1)

    def down():
        onward(1, me < peers - 2, -1)

    inside = jnp.logical_and(me > 0, me < peers - 1)

    @pl.when(jnp.logical_and(inside, me < peers // 2))
    def _():
        up()
        down()

    @pl.when(jnp.logical_and(inside, me >= peers // 2))
    def _():
        down()
        up()


def hear_word(peers, word_sem):
    me = lax.axis_index("comp")
    if peers > 2:
        for side, last in ((1, me == 0), (0, me == peers - 1)):

            @pl.when(last)
            def _(side=side):
                pl.semaphore_wait(word_sem.at[side], 1)


def send_orders(peers):
    orders = []
    for me in range(peers):
        low = me < peers // 2
        others = [t for t in range(peers) if t != me]
        across = sorted((t for t in others if (t < peers // 2) != low), key=lambda t: -abs(t - me))
        beside = sorted((t for t in others if (t < peers // 2) == low), key=lambda t: abs(t - me))
        inner = me in (peers // 2 - 1, peers // 2)
        row = across + beside if inner else beside + across
        orders.append([(t - me) % peers for t in row])
    return orders


def wave_kernel(
    peers,
    spaces,
    chunk,
    block,
    batch,
    early,
    late_first,
    late_second,
    field_ref,
    wave_in,
    substeps_in,
    trig_in,
    east_in,
    north_in,
    neighbour_in,
    quad_in,
    strength_in,
    blocks_ref,
    out_ref,
    wave_ref,
    substeps_ref,
    trig_ref,
    east_ref,
    north_ref,
    neighbour_ref,
    quad_ref,
    strength_ref,
    small_sem,
    points_ref,
    extended,
    finals,
    side_table,
    side_current,
    selector,
    currents,
    states,
    parts,
    speeds,
    repeats,
    links,
    chain,
    blocks,
    fields,
    rounded,
    products,
    slots,
    updated,
    word_sem,
    load_sem,
    blocks_sem,
    chain_sem,
    side_send,
    side_recv,
    halo_send,
    halo_recv,
    piece_send,
    piece_recv,
    home_send,
    home_recv,
    own_sem,
    turn_sem,
):
    me = lax.axis_index("comp")
    here = lax.axis_index("space")
    rows, width = field_ref.shape
    tiles = width // HALO
    reach = SUB * HALO
    chunks = rows // chunk
    has_left = here > 0
    has_right = here < spaces - 1
    odd = lax.rem(here, 2)
    goes_first = odd == jnp.where(here < spaces // 2, 0, 1)

    barrier, greetings = greet(peers, spaces)
    pairs = (
        (neighbour_in, neighbour_ref),
        (east_in, east_ref),
        (north_in, north_ref),
        (trig_in, trig_ref),
        (substeps_in, substeps_ref),
        (wave_in, wave_ref),
        (quad_in, quad_ref),
        (strength_in, strength_ref),
    )
    loads = [
        pltpu.make_async_copy(source, target, small_sem.at[i])
        for i, (source, target) in enumerate(pairs)
    ]
    for copy in loads:
        copy.start()
    load = pltpu.make_async_copy(field_ref, extended.at[:, pl.ds(reach, width)], load_sem)
    load.start()
    load_blocks = pltpu.make_async_copy(blocks_ref, blocks, blocks_sem)
    load_blocks.start()

    lane = lax.broadcasted_iota(jnp.int32, (4, HALO), 1)
    for side, missing in ((0, jnp.logical_not(has_left)), (1, jnp.logical_not(has_right))):

        @pl.when(missing)
        def _(side=side):
            first = (tiles - SUB) * HALO if side == 0 else 0
            for i in range(SUB):
                part = pl.ds(i * HALO, HALO)
                side_table[side, :, part] = lane + (first + (i + 1) * HALO)
            side_current[side] = jnp.zeros((2, 1, reach), jnp.float32)
            start = 0 if side == 0 else reach + width

            def clear(g, carry):
                at = pl.ds(pl.multiple_of(g * 8, 8), 8)
                extended[at, pl.ds(start, reach)] = jnp.zeros((8, reach), jnp.float32)
                return carry

            lax.fori_loop(0, rows // 8, clear, 0)

    def spread(row):
        return jnp.broadcast_to(row, (8, HALO))

    spot = lax.broadcasted_iota(jnp.int32, (2 * HALO, HALO), 0)

    def fill(e, table_ref, east_row, north_row, tile, place):
        for d in range(4):
            wanted = table_ref[d : d + 1, place] - (tile + d % 2) * HALO
            half = d // 2 * HALO
            chosen = jnp.where(spot == wanted, 1.0, 0.0).astype(jnp.bfloat16)
            selector[e, d % 2, :, half : half + HALO] = chosen
        currents[0, e] = spread(east_row[:, place])
        currents[1, e] = spread(north_row[:, place])

    def fill_own(j, carry):
        fill(j + SUB, neighbour_ref, east_ref, north_ref, j, pl.ds(pl.multiple_of(j * HALO, HALO), HALO))
        return carry

    for copy in loads[:3]:
        copy.wait()
    lax.fori_loop(0, tiles, fill_own, 0)

    pl.semaphore_wait(barrier, greetings)

    left = {"space": jnp.maximum(here - 1, 0)}
    right = {"space": jnp.minimum(here + 1, spaces - 1)}

    def remote(source, target, send, recv, device):
        return pltpu.make_async_remote_copy(
            src_ref=source,
            dst_ref=target,
            send_sem=send,
            recv_sem=recv,
            device_id=device,
            device_id_type=MESH,
        )

    def sides():
        copies = []
        for side, start, device in ((1, 0, left), (0, width - reach, right)):
            part = pl.ds(start, reach)
            pairs = (
                (neighbour_in.at[:, part], side_table.at[side]),
                (east_in.at[:, part], side_current.at[side, 0]),
                (north_in.at[:, part], side_current.at[side, 1]),
            )
            copies.append(
                [
                    remote(source, target, side_send.at[side, i], side_recv.at[side, i], device)
                    for i, (source, target) in enumerate(pairs)
                ]
            )
        return copies

    def halo(first, count, sem):
        part = pl.ds(first, count)
        to_left = remote(
            field_ref.at[part, pl.ds(0, reach)],
            extended.at[part, pl.ds(reach + width, reach)],
            halo_send.at[1],
            halo_recv.at[1, sem],
            left,
        )
        to_right = remote(
            field_ref.at[part, pl.ds(width - reach, reach)],
            extended.at[part, pl.ds(0, reach)],
            halo_send.at[0],
            halo_recv.at[0, sem],
            right,
        )
        return to_left, to_right

    def rows_of(c):
        return pl.multiple_of(c * chunk, 8)

    to_left_sides, to_right_sides = sides()

    @pl.when(has_left)
    def _():
        for copy in to_left_sides:
            copy.start()

    @pl.when(has_right)
    def _():
        for copy in to_right_sides:
            copy.start()

    def start_halo(c, carry):
        to_left, to_right = halo(rows_of(c), chunk, c)

        @pl.when(has_left)
        def _():
            to_left.start()

        @pl.when(has_right)
        def _():
            to_right.start()

        return carry

    lax.fori_loop(0, chunks, start_halo, 0)
    pass_word(peers, word_sem)

    @pl.when(has_right)
    def _():
        for copy in to_left_sides:
            copy.wait_recv()

    @pl.when(has_left)
    def _():
        for copy in to_right_sides:
            copy.wait_recv()

    for i in range(1, SUB):
        place = pl.ds(i * HALO, HALO)
        fill(i, side_table.at[0], side_current.at[0, 0], side_current.at[0, 1], tiles - SUB + i, place)
    for i in range(SUB - 1):
        place = pl.ds(i * HALO, HALO)
        fill(
            SUB + tiles + i, side_table.at[1], side_current.at[1, 0], side_current.at[1, 1], i, place
        )

    sublane = lax.broadcasted_iota(jnp.int32, (8, HALO), 0)
    window = block + 2 * SUB

    def prepare(first, base):
        def per_group(g, carry):
            at = pl.ds(pl.multiple_of(g * 8, 8), 8)
            component = me * rows + first + g * 8
            speed = wave_ref[component // ND]
            turn = pl.ds(pl.multiple_of(lax.rem(component, ND), 8), 8)
            own_x = trig_ref[0, turn, :] * speed
            own_y = trig_ref[1, turn, :] * speed
            taken = jnp.full((8, HALO), substeps_ref[component], jnp.int32)
            for i in range(1, 8):
                taken = jnp.where(sublane == i, substeps_ref[component + i], taken)
            count = taken.astype(jnp.float32)
            repeats[at] = count
            scale = courant_scale / count
            for i in range(1, window - 1):
                along_x = (own_x + currents[0, base + i]) * scale
                along_y = (own_y + currents[1, base + i]) * scale
                speeds[0, i, at] = jnp.clip(along_x, -courant_limit, courant_limit)
                speeds[1, i, at] = jnp.clip(along_y, -courant_limit, courant_limit)
            return carry

        lax.fori_loop(0, chunk // 8, per_group, 0)

    stacked = chunk % 16 == 0

    def pick(i, chosen):
        if stacked:
            pair = jnp.concatenate([parts[i], parts[i + 1]], axis=1)
            both = jnp.dot(pair, chosen, preferred_element_type=jnp.float32)
            taken = both[:chunk]
            for p in range(1, PARTS):
                taken = taken + both[p * chunk : (p + 1) * chunk]
        else:
            taken = None
            for p in range(PARTS):
                at = pl.ds(p * chunk, chunk)
                pair = jnp.concatenate([parts[i, at], parts[i + 1, at]], axis=1)
                term = jnp.dot(pair, chosen, preferred_element_type=jnp.float32)
                taken = term if taken is None else taken + term
        return taken[:, :HALO], taken[:, HALO:]

    def advance(first, b):
        base = b * block
        at = pl.ds(first, chunk)
        prepare(first, base)

        def state(s, i):
            if s == 0:
                return extended[at, pl.ds(pl.multiple_of((base + i) * HALO, HALO), HALO)]
            return states[s % 2, i]

        for s in range(SUB):
            for i in range(s, window - s):
                rest = state(s, i)
                for p in range(PARTS):
                    part = rest.astype(jnp.bfloat16)
                    parts[i, p * chunk : (p + 1) * chunk] = part
                    if p + 1 < PARTS:
                        rest = rest - part.astype(jnp.float32)
            for i in range(s + 1, window - 1 - s):
                value = state(s, i)
                west, south = pick(i - 1, selector[base + i, 0])
                east, north = pick(i, selector[base + i, 1])
                along_x = speeds[0, i]
                along_y = speeds[1, i]
                change = jnp.abs(along_x) * (value - jnp.where(along_x > 0.0, west, east))
                change = change + jnp.abs(along_y) * (
                    value - jnp.where(along_y > 0.0, south, north)
                )
                if s > 0:
                    change = jnp.where(repeats[...] > float(s), change, 0.0)
                if s + 1 < SUB:
                    states[(s + 1) % 2, i] = value - change
                else:
                    finals[base + i - SUB, at] = value - change

    def piece(k, first, count, group):
        target = lax.rem(me + k, peers)
        return remote(
            finals.at[target, pl.ds(first, count)],
            points_ref.at[pl.ds(pl.multiple_of(me * rows + first, 8), count)],
            piece_send.at[group, k],
            piece_recv.at[k],
            {"comp": target},
        )

    orders = send_orders(peers)
    order = []
    for place in range(peers - 1):
        k = orders[0][place]
        for other in range(1, peers):
            k = jnp.where(me == other, orders[other][place], k)
        order.append(k)
    steps = range(1, peers)
    for copy in loads[3:]:
        copy.wait()
    load.wait()

    late = jnp.where(goes_first, late_first, late_second)

    def step(c, carry):
        first = rows_of(c)
        to_left, to_right = halo(first, chunk, c)

        @pl.when(has_right)
        def _():
            to_left.wait_recv()

        @pl.when(has_left)
        def _():
            to_right.wait_recv()

        def per_block(b, inner):
            advance(first, b)
            return inner

        if tiles == block:
            advance(first, 0)
        else:
            lax.fori_loop(0, tiles // block, per_block, 0)

        @pl.when(c == 0)
        def _():
            hear_word(peers, word_sem)

        @pl.when(jnp.logical_or(goes_first, c < early))
        def _():
            for k in order:
                piece(k, first, chunk, jnp.where(c < chunks - late, 0, 1)).start()

        return carry

    lax.fori_loop(0, chunks, step, 0)
    place = pl.ds(pl.multiple_of(me * rows, 8), rows)
    own = pltpu.make_async_copy(finals.at[me], points_ref.at[place], own_sem)
    own.start()
    most_first = (chunks - late_first) * chunk
    most_second = (chunks - late_second) * chunk
    partner = {"space": here + 1 - 2 * odd}

    @pl.when(goes_first)
    def _():
        for k in steps:
            piece(k, 0, most_first, 0).wait_send()
        pl.semaphore_signal(turn_sem.at[0], inc=1, device_id=partner, device_id_type=MESH)

    @pl.when(jnp.logical_not(goes_first))
    def _():
        pl.semaphore_wait(turn_sem.at[0], 1)
        if early * chunk < most_second:
            for k in order:
                piece(k, early * chunk, most_second - early * chunk, 0).start()
        if late_second:
            for k in order:
                piece(k, most_second, rows - most_second, 1).start()
        for k in steps:
            piece(k, 0, most_second, 0).wait_send()
        pl.semaphore_signal(turn_sem.at[1], inc=1, device_id=partner, device_id_type=MESH)

    total = blocks.shape[0]
    spots = lax.broadcasted_iota(jnp.int32, (1, HALO), 1)
    none = jnp.full((1, HALO), total, jnp.int32)

    def targets(j, row):
        return jnp.where(spots == j, quad_ref[3, j], row)

    def link(j, carry):
        before, last = carry
        target = quad_ref[3, j]
        before = jnp.where(jnp.logical_and(spots > j, row == target), j, before)
        last = jnp.where(spots == target, j, last)
        return before, last

    row = lax.fori_loop(0, total, targets, none)
    before, last = lax.fori_loop(0, total, link, (none, none))
    links[0:1] = before
    links[1:2] = last
    load_chain = pltpu.make_async_copy(links, chain, chain_sem)
    load_chain.start()
    slots[total] = jnp.zeros((ND, HALO), jnp.float32)

    own.wait()
    load_blocks.wait()
    load_chain.wait()
    for k in steps:
        piece(k, 0, rows, 0).wait_recv()

    def frequency(f):
        return pl.ds(pl.multiple_of(f * ND, ND), ND)

    def take(f, carry):
        value = points_ref[frequency(f)]
        rounded[f] = value.astype(jnp.bfloat16)
        fields[f] = value
        return carry

    lax.fori_loop(0, NF, take, 0, unroll=4)

    def interact(i, carry):
        for b in range(batch):
            j = i * batch + b
            matrix = blocks[j]
            left_term = jnp.dot(matrix, rounded[quad_ref[0, j]], preferred_element_type=jnp.float32)
            right_term = lax.dot_general(
                matrix,
                rounded[quad_ref[1, j]],
                (((0,), (0,)), ((), ())),
                preferred_element_type=jnp.float32,
            )
            products[b] = (left_term * right_term * fields[quad_ref[2, j]]).astype(jnp.bfloat16)
        terms = []
        for b in range(batch):
            j = i * batch + b
            term = jnp.dot(blocks[j], products[b], preferred_element_type=jnp.float32)
            terms.append(term * (strength_ref[j] * source_step))
        for b in range(batch):
            j = i * batch + b
            slots[j] = slots[chain[0, j]] + terms[b]
        return carry

    lax.fori_loop(0, total // batch, interact, 0)

    def finish(f, carry):
        updated[frequency(f)] = fields[f] + slots[chain[1, f]]
        return carry

    lax.fori_loop(0, NF, finish, 0, unroll=4)

    @pl.when(goes_first)
    def _():
        pl.semaphore_wait(turn_sem.at[1], 1)

    column = pl.ds(pl.multiple_of(me * HALO, HALO), HALO)
    homes = []
    for k in order:
        target = lax.rem(me + k, peers)
        home = remote(
            updated.at[pl.ds(pl.multiple_of(target * rows, 8), rows)],
            out_ref.at[:, column],
            home_send.at[k],
            home_recv.at[k],
            {"comp": target},
        )
        home.start()
        homes.append(home)
    own = pltpu.make_async_copy(updated.at[place], out_ref.at[:, column], own_sem)
    own.start()
    to_left, to_right = halo(0, rows, 0)

    @pl.when(has_left)
    def _():
        to_left.wait_send()
        for copy in to_left_sides:
            copy.wait_send()

    @pl.when(has_right)
    def _():
        to_right.wait_send()
        for copy in to_right_sides:
            copy.wait_send()

    own.wait()
    for turn, most in ((goes_first, most_first), (jnp.logical_not(goes_first), most_second)):
        if most < rows:

            @pl.when(turn)
            def _(most=most):
                for k in steps:
                    piece(k, most, rows - most, 1).wait_send()

    for home in homes:
        home.wait()


def advance_waves(
    field, wave_speed, substeps, east, north, neighbours, blocks, quad_index, strength, peers, spaces
):
    rows, width = field.shape
    tiles = width // HALO
    reach = SUB * HALO
    total = blocks.shape[0]
    assert width >= reach and spaces % 2 == 0 and max(total, NF) < HALO
    chunk = chunk_rows(rows)
    block = math.gcd(tiles, 4)
    outer = tiles + 2 * SUB
    window = block + 2 * SUB
    batch = math.gcd(total, 32)
    late_first = min(LATE_FIRST, rows // chunk - 1)
    late_second = min(LATE_SECOND, rows // chunk - 1)
    early = min(EARLY, rows // chunk - late_second)
    angles = (np.arange(ND, dtype=np.float32) + np.float32(0.5)) * np.float32(2.0 * math.pi / ND)
    trig = np.stack([np.cos(angles), np.sin(angles)])
    trig = np.ascontiguousarray(np.broadcast_to(trig[:, :, None], (2, ND, HALO)))
    vmem = pl.BlockSpec(memory_space=pltpu.VMEM)
    whole = pl.BlockSpec(memory_space=pl.ANY)
    return pl.pallas_call(
        functools.partial(wave_kernel, peers, spaces, chunk, block, batch, early, late_first, late_second),
        out_shape=pltpu.VMEM((rows, width), jnp.float32),
        in_specs=[whole] * 10,
        out_specs=vmem,
        scratch_shapes=[
            pltpu.SMEM(wave_speed.shape, jnp.float32),
            pltpu.SMEM(substeps.shape, jnp.int32),
            pltpu.VMEM((2, ND, HALO), jnp.float32),
            pltpu.VMEM((1, width), jnp.float32),
            pltpu.VMEM((1, width), jnp.float32),
            pltpu.VMEM((4, width), jnp.int32),
            pltpu.SMEM(quad_index.shape, jnp.int32),
            pltpu.SMEM(strength.shape, jnp.float32),
            pltpu.SemaphoreType.DMA((8,)),
            pltpu.VMEM((peers * rows, HALO), jnp.float32),
            pltpu.VMEM((rows, width + 2 * reach), jnp.float32),
            pltpu.VMEM((tiles, rows, HALO), jnp.float32),
            pltpu.VMEM((2, 4, reach), jnp.int32),
            pltpu.VMEM((2, 2, 1, reach), jnp.float32),
            pltpu.VMEM((outer, 2, 2 * HALO, 2 * HALO), jnp.bfloat16),
            pltpu.VMEM((2, outer, 8, HALO), jnp.float32),
            pltpu.VMEM((2, window, chunk, HALO), jnp.float32),
            pltpu.VMEM((window, PARTS * chunk, HALO), jnp.bfloat16),
            pltpu.VMEM((2, window, chunk, HALO), jnp.float32),
            pltpu.VMEM((chunk, HALO), jnp.float32),
            pltpu.VMEM((8, HALO), jnp.int32),
            pltpu.SMEM((8, HALO), jnp.int32),
            pltpu.VMEM(blocks.shape, jnp.bfloat16),
            pltpu.VMEM((NF, ND, HALO), jnp.float32),
            pltpu.VMEM((NF, ND, HALO), jnp.bfloat16),
            pltpu.VMEM((batch, ND, HALO), jnp.bfloat16),
            pltpu.VMEM((total + 1, ND, HALO), jnp.float32),
            pltpu.VMEM((peers * rows, HALO), jnp.float32),
            pltpu.SemaphoreType.REGULAR((2,)),
            pltpu.SemaphoreType.DMA,
            pltpu.SemaphoreType.DMA,
            pltpu.SemaphoreType.DMA,
            pltpu.SemaphoreType.DMA((2, 3)),
            pltpu.SemaphoreType.DMA((2, 3)),
            pltpu.SemaphoreType.DMA((2,)),
            pltpu.SemaphoreType.DMA((2, rows // chunk)),
            pltpu.SemaphoreType.DMA((2, peers)),
            pltpu.SemaphoreType.DMA((peers,)),
            pltpu.SemaphoreType.DMA((peers,)),
            pltpu.SemaphoreType.DMA((peers,)),
            pltpu.SemaphoreType.DMA,
            pltpu.SemaphoreType.REGULAR((2,)),
        ],
        compiler_params=pltpu.CompilerParams(collective_id=0, has_side_effects=True),
    )(
        field,
        wave_speed,
        substeps,
        jnp.asarray(trig),
        east.reshape(1, width),
        north.reshape(1, width),
        neighbours,
        quad_index,
        strength,
        blocks,
    )


def shards(
    spectrum,
    wave_speed,
    current_east,
    current_north,
    substeps,
    neighbours,
    blocks,
    quad_index,
    strength,
):
    peers = lax.axis_size("comp")
    spaces = lax.axis_size("space")
    rows, width = spectrum.shape
    assert width == peers * HALO
    return advance_waves(
        spectrum,
        wave_speed,
        substeps,
        current_east,
        current_north,
        neighbours,
        blocks,
        quad_index,
        strength,
        peers,
        spaces,
    )


def solution(mesh):
    in_specs = (
        P("comp", ("grp", "space")),
        P(),
        P(("grp", "space")),
        P(("grp", "space")),
        P(),
        P(None, ("grp", "space")),
        P(),
        P(),
        P(),
    )
    out_specs = P("comp", ("grp", "space"))
    return jax.shard_map(shards, mesh=mesh, in_specs=in_specs, out_specs=out_specs, check_vma=False)
```

```python
import functools
import math

import jax
import jax.numpy as jnp
import numpy as np
from jax import lax
from jax.experimental import pallas as pl
from jax.experimental.pallas import tpu as pltpu
from jax.sharding import PartitionSpec as P

NF = 36
ND = 64
SUB = 4
HALO = 128
PARTS = 2
EARLY = 2
LATE_FIRST = 2
LATE_SECOND = 4

courant_scale = 0.4
courant_limit = 0.45
source_step = 0.1

MESH = pl.DeviceIdType.MESH


def chunk_rows(rows):
    for size in (64, 72, 48, 32, 24, 16, 8):
        if rows % size == 0:
            return size
    return rows


def greet(peers, spaces):
    me = lax.axis_index("comp")
    here = lax.axis_index("space")
    barrier = pltpu.get_barrier_semaphore()
    count = 0
    for axis, place, size in (("comp", me, peers), ("space", here, spaces)):
        for step, near in ((-1, place > 0), (1, place < size - 1)):

            @pl.when(near)
            def _(axis=axis, place=place, step=step):
                pl.semaphore_signal(
                    barrier, inc=1, device_id={axis: place + step}, device_id_type=MESH
                )

            count = count + jnp.where(near, 1, 0)
    return barrier, count


def pass_word(peers, word_sem):
    me = lax.axis_index("comp")

    def onward(side, waits, step):
        @pl.when(waits)
        def _():
            pl.semaphore_wait(word_sem.at[side], 1)

        pl.semaphore_signal(
            word_sem.at[side], inc=1, device_id={"comp": me + step}, device_id_type=MESH
        )

    def up():
        onward(0, me > 1, 1)

    def down():
        onward(1, me < peers - 2, -1)

    inside = jnp.logical_and(me > 0, me < peers - 1)

    @pl.when(jnp.logical_and(inside, me < peers // 2))
    def _():
        up()
        down()

    @pl.when(jnp.logical_and(inside, me >= peers // 2))
    def _():
        down()
        up()


def hear_word(peers, word_sem):
    me = lax.axis_index("comp")
    if peers > 2:
        for side, last in ((1, me == 0), (0, me == peers - 1)):

            @pl.when(last)
            def _(side=side):
                pl.semaphore_wait(word_sem.at[side], 1)


def send_orders(peers):
    orders = []
    for me in range(peers):
        low = me < peers // 2
        others = [t for t in range(peers) if t != me]
        across = sorted((t for t in others if (t < peers // 2) != low), key=lambda t: -abs(t - me))
        beside = sorted((t for t in others if (t < peers // 2) == low), key=lambda t: abs(t - me))
        inner = me in (peers // 2 - 1, peers // 2)
        row = across + beside if inner else beside + across
        orders.append([(t - me) % peers for t in row])
    return orders


def wave_kernel(
    peers,
    spaces,
    chunk,
    block,
    batch,
    early,
    late_first,
    late_second,
    field_ref,
    wave_in,
    substeps_in,
    trig_in,
    east_in,
    north_in,
    neighbour_in,
    quad_in,
    strength_in,
    blocks_ref,
    out_ref,
    wave_ref,
    substeps_ref,
    trig_ref,
    east_ref,
    north_ref,
    neighbour_ref,
    quad_ref,
    strength_ref,
    small_sem,
    points_ref,
    extended,
    finals,
    side_table,
    side_current,
    selector,
    currents,
    states,
    parts,
    speeds,
    repeats,
    links,
    chain,
    blocks,
    fields,
    rounded,
    products,
    slots,
    updated,
    word_sem,
    load_sem,
    blocks_sem,
    chain_sem,
    side_send,
    side_recv,
    halo_send,
    halo_recv,
    piece_send,
    piece_recv,
    home_send,
    home_recv,
    own_sem,
    turn_sem,
):
    me = lax.axis_index("comp")
    here = lax.axis_index("space")
    rows, width = field_ref.shape
    tiles = width // HALO
    reach = SUB * HALO
    chunks = rows // chunk
    has_left = here > 0
    has_right = here < spaces - 1
    odd = lax.rem(here, 2)
    goes_first = odd == jnp.where(here < spaces // 2, 0, 1)

    barrier, greetings = greet(peers, spaces)
    pairs = (
        (neighbour_in, neighbour_ref),
        (east_in, east_ref),
        (north_in, north_ref),
        (trig_in, trig_ref),
        (substeps_in, substeps_ref),
        (wave_in, wave_ref),
        (quad_in, quad_ref),
        (strength_in, strength_ref),
    )
    loads = [
        pltpu.make_async_copy(source, target, small_sem.at[i])
        for i, (source, target) in enumerate(pairs)
    ]
    for copy in loads:
        copy.start()
    load = pltpu.make_async_copy(field_ref, extended.at[:, pl.ds(reach, width)], load_sem)
    load.start()
    load_blocks = pltpu.make_async_copy(blocks_ref, blocks, blocks_sem)
    load_blocks.start()

    lane = lax.broadcasted_iota(jnp.int32, (4, HALO), 1)
    for side, missing in ((0, jnp.logical_not(has_left)), (1, jnp.logical_not(has_right))):

        @pl.when(missing)
        def _(side=side):
            first = (tiles - SUB) * HALO if side == 0 else 0
            for i in range(SUB):
                part = pl.ds(i * HALO, HALO)
                side_table[side, :, part] = lane + (first + (i + 1) * HALO)
            side_current[side] = jnp.zeros((2, 1, reach), jnp.float32)
            start = 0 if side == 0 else reach + width

            def clear(g, carry):
                at = pl.ds(pl.multiple_of(g * 8, 8), 8)
                extended[at, pl.ds(start, reach)] = jnp.zeros((8, reach), jnp.float32)
                return carry

            lax.fori_loop(0, rows // 8, clear, 0)

    def spread(row):
        return jnp.broadcast_to(row, (8, HALO))

    spot = lax.broadcasted_iota(jnp.int32, (2 * HALO, HALO), 0)

    def fill(e, table_ref, east_row, north_row, tile, place):
        for d in range(4):
            wanted = table_ref[d : d + 1, place] - (tile + d % 2) * HALO
            half = d // 2 * HALO
            chosen = jnp.where(spot == wanted, 1.0, 0.0).astype(jnp.bfloat16)
            selector[e, d % 2, :, half : half + HALO] = chosen
        currents[0, e] = spread(east_row[:, place])
        currents[1, e] = spread(north_row[:, place])

    def fill_own(j, carry):
        fill(j + SUB, neighbour_ref, east_ref, north_ref, j, pl.ds(pl.multiple_of(j * HALO, HALO), HALO))
        return carry

    for copy in loads[:3]:
        copy.wait()
    lax.fori_loop(0, tiles, fill_own, 0)

    pl.semaphore_wait(barrier, greetings)

    left = {"space": jnp.maximum(here - 1, 0)}
    right = {"space": jnp.minimum(here + 1, spaces - 1)}

    def remote(source, target, send, recv, device):
        return pltpu.make_async_remote_copy(
            src_ref=source,
            dst_ref=target,
            send_sem=send,
            recv_sem=recv,
            device_id=device,
            device_id_type=MESH,
        )

    def sides():
        copies = []
        for side, start, device in ((1, 0, left), (0, width - reach, right)):
            part = pl.ds(start, reach)
            pairs = (
                (neighbour_in.at[:, part], side_table.at[side]),
                (east_in.at[:, part], side_current.at[side, 0]),
                (north_in.at[:, part], side_current.at[side, 1]),
            )
            copies.append(
                [
                    remote(source, target, side_send.at[side, i], side_recv.at[side, i], device)
                    for i, (source, target) in enumerate(pairs)
                ]
            )
        return copies

    def halo(first, count, sem):
        part = pl.ds(first, count)
        to_left = remote(
            field_ref.at[part, pl.ds(0, reach)],
            extended.at[part, pl.ds(reach + width, reach)],
            halo_send.at[1],
            halo_recv.at[1, sem],
            left,
        )
        to_right = remote(
            field_ref.at[part, pl.ds(width - reach, reach)],
            extended.at[part, pl.ds(0, reach)],
            halo_send.at[0],
            halo_recv.at[0, sem],
            right,
        )
        return to_left, to_right

    def rows_of(c):
        return pl.multiple_of(c * chunk, 8)

    to_left_sides, to_right_sides = sides()

    @pl.when(has_left)
    def _():
        for copy in to_left_sides:
            copy.start()

    @pl.when(has_right)
    def _():
        for copy in to_right_sides:
            copy.start()

    def start_halo(c, carry):
        to_left, to_right = halo(rows_of(c), chunk, c)

        @pl.when(has_left)
        def _():
            to_left.start()

        @pl.when(has_right)
        def _():
            to_right.start()

        return carry

    lax.fori_loop(0, chunks, start_halo, 0)
    pass_word(peers, word_sem)

    @pl.when(has_right)
    def _():
        for copy in to_left_sides:
            copy.wait_recv()

    @pl.when(has_left)
    def _():
        for copy in to_right_sides:
            copy.wait_recv()

    trimmed = tiles == block

    @pl.when(jnp.logical_or(has_left, not trimmed))
    def _():
        for i in range(1, SUB):
            place = pl.ds(i * HALO, HALO)
            east_row, north_row = side_current.at[0, 0], side_current.at[0, 1]
            fill(i, side_table.at[0], east_row, north_row, tiles - SUB + i, place)

    @pl.when(jnp.logical_or(has_right, not trimmed))
    def _():
        for i in range(SUB - 1):
            place = pl.ds(i * HALO, HALO)
            east_row, north_row = side_current.at[1, 0], side_current.at[1, 1]
            fill(SUB + tiles + i, side_table.at[1], east_row, north_row, i, place)

    sublane = lax.broadcasted_iota(jnp.int32, (8, HALO), 0)
    window = block + 2 * SUB

    def prepare(first, base, low, high):
        def per_group(g, carry):
            at = pl.ds(pl.multiple_of(g * 8, 8), 8)
            component = me * rows + first + g * 8
            speed = wave_ref[component // ND]
            turn = pl.ds(pl.multiple_of(lax.rem(component, ND), 8), 8)
            own_x = trig_ref[0, turn, :] * speed
            own_y = trig_ref[1, turn, :] * speed
            taken = jnp.full((8, HALO), substeps_ref[component], jnp.int32)
            for i in range(1, 8):
                taken = jnp.where(sublane == i, substeps_ref[component + i], taken)
            count = taken.astype(jnp.float32)
            repeats[at] = count
            scale = courant_scale / count
            for i in range(low, high):
                along_x = (own_x + currents[0, base + i]) * scale
                along_y = (own_y + currents[1, base + i]) * scale
                speeds[0, i, at] = jnp.clip(along_x, -courant_limit, courant_limit)
                speeds[1, i, at] = jnp.clip(along_y, -courant_limit, courant_limit)
            return carry

        lax.fori_loop(0, chunk // 8, per_group, 0)

    stacked = chunk % 16 == 0

    def pick(i, chosen):
        if stacked:
            pair = jnp.concatenate([parts[i], parts[i + 1]], axis=1)
            both = jnp.dot(pair, chosen, preferred_element_type=jnp.float32)
            taken = both[:chunk]
            for p in range(1, PARTS):
                taken = taken + both[p * chunk : (p + 1) * chunk]
        else:
            taken = None
            for p in range(PARTS):
                at = pl.ds(p * chunk, chunk)
                pair = jnp.concatenate([parts[i, at], parts[i + 1, at]], axis=1)
                term = jnp.dot(pair, chosen, preferred_element_type=jnp.float32)
                taken = term if taken is None else taken + term
        return taken[:, :HALO], taken[:, HALO:]

    def advance(first, b, open_left=True, open_right=True):
        base = b * block
        at = pl.ds(first, chunk)
        low = 0 if open_left else SUB - 1
        high = window if open_right else window - SUB + 1
        prepare(first, base, low + 1, high - 1)

        def state(s, i):
            if s == 0:
                return extended[at, pl.ds(pl.multiple_of((base + i) * HALO, HALO), HALO)]
            return states[s % 2, i]

        for s in range(SUB):
            edge = min(s, 1)
            for i in range(max(s, low + edge), min(window - s, high - edge)):
                rest = state(s, i)
                for p in range(PARTS):
                    part = rest.astype(jnp.bfloat16)
                    parts[i, p * chunk : (p + 1) * chunk] = part
                    if p + 1 < PARTS:
                        rest = rest - part.astype(jnp.float32)
            for i in range(max(s, low) + 1, min(window - s, high) - 1):
                value = state(s, i)
                west, south = pick(i - 1, selector[base + i, 0])
                east, north = pick(i, selector[base + i, 1])
                along_x = speeds[0, i]
                along_y = speeds[1, i]
                change = jnp.abs(along_x) * (value - jnp.where(along_x > 0.0, west, east))
                change = change + jnp.abs(along_y) * (
                    value - jnp.where(along_y > 0.0, south, north)
                )
                if s > 0:
                    change = jnp.where(repeats[...] > float(s), change, 0.0)
                if s + 1 < SUB:
                    states[(s + 1) % 2, i] = value - change
                else:
                    finals[base + i - SUB, at] = value - change

    def piece(k, first, count, group):
        target = lax.rem(me + k, peers)
        return remote(
            finals.at[target, pl.ds(first, count)],
            points_ref.at[pl.ds(pl.multiple_of(me * rows + first, 8), count)],
            piece_send.at[group, k],
            piece_recv.at[k],
            {"comp": target},
        )

    orders = send_orders(peers)
    order = []
    for place in range(peers - 1):
        k = orders[0][place]
        for other in range(1, peers):
            k = jnp.where(me == other, orders[other][place], k)
        order.append(k)
    steps = range(1, peers)
    for copy in loads[3:]:
        copy.wait()
    load.wait()

    late = jnp.where(goes_first, late_first, late_second)

    def step(c, carry):
        first = rows_of(c)
        to_left, to_right = halo(first, chunk, c)

        @pl.when(has_right)
        def _():
            to_left.wait_recv()

        @pl.when(has_left)
        def _():
            to_right.wait_recv()

        def per_block(b, inner):
            advance(first, b)
            return inner

        if trimmed:

            @pl.when(jnp.logical_and(has_left, has_right))
            def _():
                advance(first, 0)

            @pl.when(jnp.logical_not(has_left))
            def _():
                advance(first, 0, open_left=False)

            @pl.when(jnp.logical_not(has_right))
            def _():
                advance(first, 0, open_right=False)

        else:
            lax.fori_loop(0, tiles // block, per_block, 0)

        @pl.when(c == 0)
        def _():
            hear_word(peers, word_sem)

        @pl.when(jnp.logical_or(goes_first, c < early))
        def _():
            for k in order:
                piece(k, first, chunk, jnp.where(c < chunks - late, 0, 1)).start()

        return carry

    lax.fori_loop(0, chunks, step, 0)
    place = pl.ds(pl.multiple_of(me * rows, 8), rows)
    own = pltpu.make_async_copy(finals.at[me], points_ref.at[place], own_sem)
    own.start()
    most_first = (chunks - late_first) * chunk
    most_second = (chunks - late_second) * chunk
    partner = {"space": here + 1 - 2 * odd}

    @pl.when(goes_first)
    def _():
        for k in steps:
            piece(k, 0, most_first, 0).wait_send()
        pl.semaphore_signal(turn_sem.at[0], inc=1, device_id=partner, device_id_type=MESH)

    @pl.when(jnp.logical_not(goes_first))
    def _():
        pl.semaphore_wait(turn_sem.at[0], 1)
        if early * chunk < most_second:
            for k in order:
                piece(k, early * chunk, most_second - early * chunk, 0).start()
        if late_second:
            for k in order:
                piece(k, most_second, rows - most_second, 1).start()
        for k in steps:
            piece(k, 0, most_second, 0).wait_send()
        pl.semaphore_signal(turn_sem.at[1], inc=1, device_id=partner, device_id_type=MESH)

    total = blocks.shape[0]
    spots = lax.broadcasted_iota(jnp.int32, (1, HALO), 1)
    none = jnp.full((1, HALO), total, jnp.int32)

    def targets(j, row):
        return jnp.where(spots == j, quad_ref[3, j], row)

    def link(j, carry):
        before, last = carry
        target = quad_ref[3, j]
        before = jnp.where(jnp.logical_and(spots > j, row == target), j, before)
        last = jnp.where(spots == target, j, last)
        return before, last

    row = lax.fori_loop(0, total, targets, none)
    before, last = lax.fori_loop(0, total, link, (none, none))
    links[0:1] = before
    links[1:2] = last
    load_chain = pltpu.make_async_copy(links, chain, chain_sem)
    load_chain.start()
    slots[total] = jnp.zeros((ND, HALO), jnp.float32)

    own.wait()
    load_blocks.wait()
    load_chain.wait()
    for k in steps:
        piece(k, 0, rows, 0).wait_recv()

    def frequency(f):
        return pl.ds(pl.multiple_of(f * ND, ND), ND)

    def take(f, carry):
        value = points_ref[frequency(f)]
        rounded[f] = value.astype(jnp.bfloat16)
        fields[f] = value
        return carry

    lax.fori_loop(0, NF, take, 0, unroll=4)

    def interact(i, carry):
        for b in range(batch):
            j = i * batch + b
            matrix = blocks[j]
            left_term = jnp.dot(matrix, rounded[quad_ref[0, j]], preferred_element_type=jnp.float32)
            right_term = lax.dot_general(
                matrix,
                rounded[quad_ref[1, j]],
                (((0,), (0,)), ((), ())),
                preferred_element_type=jnp.float32,
            )
            products[b] = (left_term * right_term * fields[quad_ref[2, j]]).astype(jnp.bfloat16)
        terms = []
        for b in range(batch):
            j = i * batch + b
            term = jnp.dot(blocks[j], products[b], preferred_element_type=jnp.float32)
            terms.append(term * (strength_ref[j] * source_step))
        for b in range(batch):
            j = i * batch + b
            slots[j] = slots[chain[0, j]] + terms[b]
        return carry

    lax.fori_loop(0, total // batch, interact, 0)

    def finish(f, carry):
        updated[frequency(f)] = fields[f] + slots[chain[1, f]]
        return carry

    lax.fori_loop(0, NF, finish, 0, unroll=4)

    @pl.when(goes_first)
    def _():
        pl.semaphore_wait(turn_sem.at[1], 1)

    column = pl.ds(pl.multiple_of(me * HALO, HALO), HALO)
    homes = []
    for k in order:
        target = lax.rem(me + k, peers)
        home = remote(
            updated.at[pl.ds(pl.multiple_of(target * rows, 8), rows)],
            out_ref.at[:, column],
            home_send.at[k],
            home_recv.at[k],
            {"comp": target},
        )
        home.start()
        homes.append(home)
    own = pltpu.make_async_copy(updated.at[place], out_ref.at[:, column], own_sem)
    own.start()
    to_left, to_right = halo(0, rows, 0)

    @pl.when(has_left)
    def _():
        to_left.wait_send()
        for copy in to_left_sides:
            copy.wait_send()

    @pl.when(has_right)
    def _():
        to_right.wait_send()
        for copy in to_right_sides:
            copy.wait_send()

    own.wait()
    for turn, most in ((goes_first, most_first), (jnp.logical_not(goes_first), most_second)):
        if most < rows:

            @pl.when(turn)
            def _(most=most):
                for k in steps:
                    piece(k, most, rows - most, 1).wait_send()

    for home in homes:
        home.wait()


def advance_waves(
    field, wave_speed, substeps, east, north, neighbours, blocks, quad_index, strength, peers, spaces
):
    rows, width = field.shape
    tiles = width // HALO
    reach = SUB * HALO
    total = blocks.shape[0]
    assert width >= reach and spaces % 2 == 0 and max(total, NF) < HALO
    chunk = chunk_rows(rows)
    block = math.gcd(tiles, 4)
    outer = tiles + 2 * SUB
    window = block + 2 * SUB
    batch = math.gcd(total, 32)
    late_first = min(LATE_FIRST, rows // chunk - 1)
    late_second = min(LATE_SECOND, rows // chunk - 1)
    early = min(EARLY, rows // chunk - late_second)
    angles = (np.arange(ND, dtype=np.float32) + np.float32(0.5)) * np.float32(2.0 * math.pi / ND)
    trig = np.stack([np.cos(angles), np.sin(angles)])
    trig = np.ascontiguousarray(np.broadcast_to(trig[:, :, None], (2, ND, HALO)))
    vmem = pl.BlockSpec(memory_space=pltpu.VMEM)
    whole = pl.BlockSpec(memory_space=pl.ANY)
    return pl.pallas_call(
        functools.partial(wave_kernel, peers, spaces, chunk, block, batch, early, late_first, late_second),
        out_shape=pltpu.VMEM((rows, width), jnp.float32),
        in_specs=[whole] * 10,
        out_specs=vmem,
        scratch_shapes=[
            pltpu.SMEM(wave_speed.shape, jnp.float32),
            pltpu.SMEM(substeps.shape, jnp.int32),
            pltpu.VMEM((2, ND, HALO), jnp.float32),
            pltpu.VMEM((1, width), jnp.float32),
            pltpu.VMEM((1, width), jnp.float32),
            pltpu.VMEM((4, width), jnp.int32),
            pltpu.SMEM(quad_index.shape, jnp.int32),
            pltpu.SMEM(strength.shape, jnp.float32),
            pltpu.SemaphoreType.DMA((8,)),
            pltpu.VMEM((peers * rows, HALO), jnp.float32),
            pltpu.VMEM((rows, width + 2 * reach), jnp.float32),
            pltpu.VMEM((tiles, rows, HALO), jnp.float32),
            pltpu.VMEM((2, 4, reach), jnp.int32),
            pltpu.VMEM((2, 2, 1, reach), jnp.float32),
            pltpu.VMEM((outer, 2, 2 * HALO, 2 * HALO), jnp.bfloat16),
            pltpu.VMEM((2, outer, 8, HALO), jnp.float32),
            pltpu.VMEM((2, window, chunk, HALO), jnp.float32),
            pltpu.VMEM((window, PARTS * chunk, HALO), jnp.bfloat16),
            pltpu.VMEM((2, window, chunk, HALO), jnp.float32),
            pltpu.VMEM((chunk, HALO), jnp.float32),
            pltpu.VMEM((8, HALO), jnp.int32),
            pltpu.SMEM((8, HALO), jnp.int32),
            pltpu.VMEM(blocks.shape, jnp.bfloat16),
            pltpu.VMEM((NF, ND, HALO), jnp.float32),
            pltpu.VMEM((NF, ND, HALO), jnp.bfloat16),
            pltpu.VMEM((batch, ND, HALO), jnp.bfloat16),
            pltpu.VMEM((total + 1, ND, HALO), jnp.float32),
            pltpu.VMEM((peers * rows, HALO), jnp.float32),
            pltpu.SemaphoreType.REGULAR((2,)),
            pltpu.SemaphoreType.DMA,
            pltpu.SemaphoreType.DMA,
            pltpu.SemaphoreType.DMA,
            pltpu.SemaphoreType.DMA((2, 3)),
            pltpu.SemaphoreType.DMA((2, 3)),
            pltpu.SemaphoreType.DMA((2,)),
            pltpu.SemaphoreType.DMA((2, rows // chunk)),
            pltpu.SemaphoreType.DMA((2, peers)),
            pltpu.SemaphoreType.DMA((peers,)),
            pltpu.SemaphoreType.DMA((peers,)),
            pltpu.SemaphoreType.DMA((peers,)),
            pltpu.SemaphoreType.DMA,
            pltpu.SemaphoreType.REGULAR((2,)),
        ],
        compiler_params=pltpu.CompilerParams(collective_id=0, has_side_effects=True),
    )(
        field,
        wave_speed,
        substeps,
        jnp.asarray(trig),
        east.reshape(1, width),
        north.reshape(1, width),
        neighbours,
        quad_index,
        strength,
        blocks,
    )


def shards(
    spectrum,
    wave_speed,
    current_east,
    current_north,
    substeps,
    neighbours,
    blocks,
    quad_index,
    strength,
):
    peers = lax.axis_size("comp")
    spaces = lax.axis_size("space")
    rows, width = spectrum.shape
    assert width == peers * HALO
    return advance_waves(
        spectrum,
        wave_speed,
        substeps,
        current_east,
        current_north,
        neighbours,
        blocks,
        quad_index,
        strength,
        peers,
        spaces,
    )


def solution(mesh):
    in_specs = (
        P("comp", ("grp", "space")),
        P(),
        P(("grp", "space")),
        P(("grp", "space")),
        P(),
        P(None, ("grp", "space")),
        P(),
        P(),
        P(),
    )
    out_specs = P("comp", ("grp", "space"))
    return jax.shard_map(shards, mesh=mesh, in_specs=in_specs, out_specs=out_specs, check_vma=False)
```

```python
import functools
import math

import jax
import jax.numpy as jnp
import numpy as np
from jax import lax
from jax.experimental import pallas as pl
from jax.experimental.pallas import tpu as pltpu
from jax.sharding import PartitionSpec as P

NF = 36
ND = 64
SUB = 4
HALO = 128
PARTS = 2
EARLY = 2
LATE_FIRST = 2
LATE_SECOND = 4

courant_scale = 0.4
courant_limit = 0.45
source_step = 0.1

MESH = pl.DeviceIdType.MESH


def chunk_rows(rows):
    for size in (64, 72, 48, 32, 24, 16, 8):
        if rows % size == 0:
            return size
    return rows


def greet(peers, spaces):
    me = lax.axis_index("comp")
    here = lax.axis_index("space")
    barrier = pltpu.get_barrier_semaphore()
    count = 0
    for axis, place, size in (("comp", me, peers), ("space", here, spaces)):
        for step, near in ((-1, place > 0), (1, place < size - 1)):

            @pl.when(near)
            def _(axis=axis, place=place, step=step):
                pl.semaphore_signal(
                    barrier, inc=1, device_id={axis: place + step}, device_id_type=MESH
                )

            count = count + jnp.where(near, 1, 0)
    return barrier, count


def pass_word(peers, word_sem):
    me = lax.axis_index("comp")

    def onward(side, waits, step):
        @pl.when(waits)
        def _():
            pl.semaphore_wait(word_sem.at[side], 1)

        pl.semaphore_signal(
            word_sem.at[side], inc=1, device_id={"comp": me + step}, device_id_type=MESH
        )

    def up():
        onward(0, me > 1, 1)

    def down():
        onward(1, me < peers - 2, -1)

    inside = jnp.logical_and(me > 0, me < peers - 1)

    @pl.when(jnp.logical_and(inside, me < peers // 2))
    def _():
        up()
        down()

    @pl.when(jnp.logical_and(inside, me >= peers // 2))
    def _():
        down()
        up()


def hear_word(peers, word_sem):
    me = lax.axis_index("comp")
    if peers > 2:
        for side, last in ((1, me == 0), (0, me == peers - 1)):

            @pl.when(last)
            def _(side=side):
                pl.semaphore_wait(word_sem.at[side], 1)


def send_orders(peers):
    orders = []
    for me in range(peers):
        low = me < peers // 2
        others = [t for t in range(peers) if t != me]
        across = sorted((t for t in others if (t < peers // 2) != low), key=lambda t: -abs(t - me))
        beside = sorted((t for t in others if (t < peers // 2) == low), key=lambda t: abs(t - me))
        inner = me in (peers // 2 - 1, peers // 2)
        row = across + beside if inner else beside + across
        orders.append([(t - me) % peers for t in row])
    return orders


def wave_kernel(
    peers,
    spaces,
    chunk,
    block,
    batch,
    early,
    late_first,
    late_second,
    field_ref,
    wave_in,
    substeps_in,
    trig_in,
    east_in,
    north_in,
    neighbour_in,
    quad_in,
    strength_in,
    blocks_ref,
    out_ref,
    wave_ref,
    substeps_ref,
    trig_ref,
    east_ref,
    north_ref,
    neighbour_ref,
    quad_ref,
    strength_ref,
    small_sem,
    points_ref,
    extended,
    finals,
    side_table,
    side_current,
    selector,
    currents,
    states,
    parts,
    speeds,
    repeats,
    links,
    chain,
    blocks,
    fields,
    rounded,
    products,
    slots,
    updated,
    word_sem,
    load_sem,
    blocks_sem,
    chain_sem,
    side_send,
    side_recv,
    halo_send,
    halo_recv,
    piece_send,
    piece_recv,
    home_send,
    home_recv,
    own_sem,
    turn_sem,
):
    me = lax.axis_index("comp")
    here = lax.axis_index("space")
    rows, width = field_ref.shape
    tiles = width // HALO
    reach = SUB * HALO
    chunks = rows // chunk
    has_left = here > 0
    has_right = here < spaces - 1
    odd = lax.rem(here, 2)
    goes_first = odd == jnp.where(here < spaces // 2, 0, 1)

    barrier, greetings = greet(peers, spaces)
    pairs = (
        (neighbour_in, neighbour_ref),
        (east_in, east_ref),
        (north_in, north_ref),
        (trig_in, trig_ref),
        (substeps_in, substeps_ref),
        (wave_in, wave_ref),
        (quad_in, quad_ref),
        (strength_in, strength_ref),
    )
    loads = [
        pltpu.make_async_copy(source, target, small_sem.at[i])
        for i, (source, target) in enumerate(pairs)
    ]
    for copy in loads:
        copy.start()
    load = pltpu.make_async_copy(field_ref, extended.at[:, pl.ds(reach, width)], load_sem)
    load.start()
    load_blocks = pltpu.make_async_copy(blocks_ref, blocks, blocks_sem)
    load_blocks.start()

    lane = lax.broadcasted_iota(jnp.int32, (4, HALO), 1)
    for side, missing in ((0, jnp.logical_not(has_left)), (1, jnp.logical_not(has_right))):

        @pl.when(missing)
        def _(side=side):
            first = (tiles - SUB) * HALO if side == 0 else 0
            for i in range(SUB):
                part = pl.ds(i * HALO, HALO)
                side_table[side, :, part] = lane + (first + (i + 1) * HALO)
            side_current[side] = jnp.zeros((2, 1, reach), jnp.float32)
            start = 0 if side == 0 else reach + width

            def clear(g, carry):
                at = pl.ds(pl.multiple_of(g * 8, 8), 8)
                extended[at, pl.ds(start, reach)] = jnp.zeros((8, reach), jnp.float32)
                return carry

            lax.fori_loop(0, rows // 8, clear, 0)

    def spread(row):
        return jnp.broadcast_to(row, (8, HALO))

    spot = lax.broadcasted_iota(jnp.int32, (2 * HALO, HALO), 0)

    def fill(e, table_ref, east_row, north_row, tile, place):
        for d in range(4):
            wanted = table_ref[d : d + 1, place] - (tile + d % 2) * HALO
            half = d // 2 * HALO
            chosen = jnp.where(spot == wanted, 1.0, 0.0).astype(jnp.bfloat16)
            selector[e, d % 2, :, half : half + HALO] = chosen
        currents[0, e] = spread(east_row[:, place])
        currents[1, e] = spread(north_row[:, place])

    def fill_own(j, carry):
        fill(j + SUB, neighbour_ref, east_ref, north_ref, j, pl.ds(pl.multiple_of(j * HALO, HALO), HALO))
        return carry

    for copy in loads[:3]:
        copy.wait()
    lax.fori_loop(0, tiles, fill_own, 0)

    pl.semaphore_wait(barrier, greetings)

    left = {"space": jnp.maximum(here - 1, 0)}
    right = {"space": jnp.minimum(here + 1, spaces - 1)}

    def remote(source, target, send, recv, device):
        return pltpu.make_async_remote_copy(
            src_ref=source,
            dst_ref=target,
            send_sem=send,
            recv_sem=recv,
            device_id=device,
            device_id_type=MESH,
        )

    def sides():
        copies = []
        for side, start, device in ((1, 0, left), (0, width - reach, right)):
            part = pl.ds(start, reach)
            pairs = (
                (neighbour_in.at[:, part], side_table.at[side]),
                (east_in.at[:, part], side_current.at[side, 0]),
                (north_in.at[:, part], side_current.at[side, 1]),
            )
            copies.append(
                [
                    remote(source, target, side_send.at[side, i], side_recv.at[side, i], device)
                    for i, (source, target) in enumerate(pairs)
                ]
            )
        return copies

    def halo(first, count, sem):
        part = pl.ds(first, count)
        to_left = remote(
            field_ref.at[part, pl.ds(0, reach)],
            extended.at[part, pl.ds(reach + width, reach)],
            halo_send.at[1],
            halo_recv.at[1, sem],
            left,
        )
        to_right = remote(
            field_ref.at[part, pl.ds(width - reach, reach)],
            extended.at[part, pl.ds(0, reach)],
            halo_send.at[0],
            halo_recv.at[0, sem],
            right,
        )
        return to_left, to_right

    def rows_of(c):
        return pl.multiple_of(c * chunk, 8)

    to_left_sides, to_right_sides = sides()

    @pl.when(has_left)
    def _():
        for copy in to_left_sides:
            copy.start()

    @pl.when(has_right)
    def _():
        for copy in to_right_sides:
            copy.start()

    def start_halo(c, carry):
        to_left, to_right = halo(rows_of(c), chunk, c)

        @pl.when(has_left)
        def _():
            to_left.start()

        @pl.when(has_right)
        def _():
            to_right.start()

        return carry

    lax.fori_loop(0, chunks, start_halo, 0)
    pass_word(peers, word_sem)

    @pl.when(has_right)
    def _():
        for copy in to_left_sides:
            copy.wait_recv()

    @pl.when(has_left)
    def _():
        for copy in to_right_sides:
            copy.wait_recv()

    trimmed = tiles == block

    @pl.when(jnp.logical_or(has_left, not trimmed))
    def _():
        for i in range(1, SUB):
            place = pl.ds(i * HALO, HALO)
            east_row, north_row = side_current.at[0, 0], side_current.at[0, 1]
            fill(i, side_table.at[0], east_row, north_row, tiles - SUB + i, place)

    @pl.when(jnp.logical_or(has_right, not trimmed))
    def _():
        for i in range(SUB - 1):
            place = pl.ds(i * HALO, HALO)
            east_row, north_row = side_current.at[1, 0], side_current.at[1, 1]
            fill(SUB + tiles + i, side_table.at[1], east_row, north_row, i, place)

    sublane = lax.broadcasted_iota(jnp.int32, (8, HALO), 0)
    window = block + 2 * SUB

    def prepare(first, base, low, high):
        def per_group(g, carry):
            at = pl.ds(pl.multiple_of(g * 8, 8), 8)
            component = me * rows + first + g * 8
            speed = wave_ref[component // ND]
            turn = pl.ds(pl.multiple_of(lax.rem(component, ND), 8), 8)
            own_x = trig_ref[0, turn, :] * speed
            own_y = trig_ref[1, turn, :] * speed
            taken = jnp.full((8, HALO), substeps_ref[component], jnp.int32)
            for i in range(1, 8):
                taken = jnp.where(sublane == i, substeps_ref[component + i], taken)
            count = taken.astype(jnp.float32)
            repeats[at] = count
            scale = courant_scale / count
            for i in range(low, high):
                along_x = (own_x + currents[0, base + i]) * scale
                along_y = (own_y + currents[1, base + i]) * scale
                speeds[0, i, at] = jnp.clip(along_x, -courant_limit, courant_limit)
                speeds[1, i, at] = jnp.clip(along_y, -courant_limit, courant_limit)
            return carry

        lax.fori_loop(0, chunk // 8, per_group, 0)

    stacked = chunk % 16 == 0

    def pick(i, chosen):
        if stacked:
            pair = jnp.concatenate([parts[i], parts[i + 1]], axis=1)
            both = jnp.dot(pair, chosen, preferred_element_type=jnp.float32)
            taken = both[:chunk]
            for p in range(1, PARTS):
                taken = taken + both[p * chunk : (p + 1) * chunk]
        else:
            taken = None
            for p in range(PARTS):
                at = pl.ds(p * chunk, chunk)
                pair = jnp.concatenate([parts[i, at], parts[i + 1, at]], axis=1)
                term = jnp.dot(pair, chosen, preferred_element_type=jnp.float32)
                taken = term if taken is None else taken + term
        return taken[:, :HALO], taken[:, HALO:]

    def advance(first, b, open_left=True, open_right=True):
        base = b * block
        at = pl.ds(first, chunk)
        low = 0 if open_left else SUB - 1
        high = window if open_right else window - SUB + 1
        prepare(first, base, low + 1, high - 1)

        def state(s, i):
            if s == 0:
                return extended[at, pl.ds(pl.multiple_of((base + i) * HALO, HALO), HALO)]
            return states[s % 2, i]

        for s in range(SUB):
            edge = min(s, 1)
            for i in range(max(s, low + edge), min(window - s, high - edge)):
                rest = state(s, i)
                for p in range(PARTS):
                    part = rest.astype(jnp.bfloat16)
                    parts[i, p * chunk : (p + 1) * chunk] = part
                    if p + 1 < PARTS:
                        rest = rest - part.astype(jnp.float32)
            for i in range(max(s, low) + 1, min(window - s, high) - 1):
                value = state(s, i)
                west, south = pick(i - 1, selector[base + i, 0])
                east, north = pick(i, selector[base + i, 1])
                along_x = speeds[0, i]
                along_y = speeds[1, i]
                change = jnp.abs(along_x) * (value - jnp.where(along_x > 0.0, west, east))
                change = change + jnp.abs(along_y) * (
                    value - jnp.where(along_y > 0.0, south, north)
                )
                if s > 0:
                    change = jnp.where(repeats[...] > float(s), change, 0.0)
                if s + 1 < SUB:
                    states[(s + 1) % 2, i] = value - change
                else:
                    finals[base + i - SUB, at] = value - change

    def piece(k, first, count, group):
        target = lax.rem(me + k, peers)
        return remote(
            finals.at[target, pl.ds(first, count)],
            points_ref.at[pl.ds(pl.multiple_of(me * rows + first, 8), count)],
            piece_send.at[group, k],
            piece_recv.at[k],
            {"comp": target},
        )

    orders = send_orders(peers)
    order = []
    for place in range(peers - 1):
        k = orders[0][place]
        for other in range(1, peers):
            k = jnp.where(me == other, orders[other][place], k)
        order.append(k)
    steps = range(1, peers)
    for copy in loads[3:]:
        copy.wait()
    load.wait()

    late = jnp.where(goes_first, late_first, late_second)

    def step(c, carry):
        first = rows_of(c)
        to_left, to_right = halo(first, chunk, c)

        @pl.when(has_right)
        def _():
            to_left.wait_recv()

        @pl.when(has_left)
        def _():
            to_right.wait_recv()

        def per_block(b, inner):
            advance(first, b)
            return inner

        if trimmed:

            @pl.when(jnp.logical_and(has_left, has_right))
            def _():
                advance(first, 0)

            @pl.when(jnp.logical_not(has_left))
            def _():
                advance(first, 0, open_left=False)

            @pl.when(jnp.logical_not(has_right))
            def _():
                advance(first, 0, open_right=False)

        else:
            lax.fori_loop(0, tiles // block, per_block, 0)

        @pl.when(c == 0)
        def _():
            hear_word(peers, word_sem)

        @pl.when(jnp.logical_or(goes_first, c < early))
        def _():
            for k in order:
                piece(k, first, chunk, jnp.where(c < chunks - late, 0, 1)).start()

        return carry

    lax.fori_loop(0, chunks, step, 0)
    place = pl.ds(pl.multiple_of(me * rows, 8), rows)
    own = pltpu.make_async_copy(finals.at[me], points_ref.at[place], own_sem)
    own.start()
    most_first = (chunks - late_first) * chunk
    most_second = (chunks - late_second) * chunk
    partner = {"space": here + 1 - 2 * odd}

    @pl.when(goes_first)
    def _():
        for k in steps:
            piece(k, 0, most_first, 0).wait_send()
        pl.semaphore_signal(turn_sem.at[0], inc=1, device_id=partner, device_id_type=MESH)

    @pl.when(jnp.logical_not(goes_first))
    def _():
        pl.semaphore_wait(turn_sem.at[0], 1)
        if early * chunk < most_second:
            for k in order:
                piece(k, early * chunk, most_second - early * chunk, 0).start()
        if late_second:
            for k in order:
                piece(k, most_second, rows - most_second, 1).start()
        for k in steps:
            piece(k, 0, most_second, 0).wait_send()
        pl.semaphore_signal(turn_sem.at[1], inc=1, device_id=partner, device_id_type=MESH)

    total = blocks.shape[0]
    spots = lax.broadcasted_iota(jnp.int32, (1, HALO), 1)
    none = jnp.full((1, HALO), total, jnp.int32)

    def targets(j, row):
        return jnp.where(spots == j, quad_ref[3, j], row)

    def link(j, carry):
        before, last = carry
        target = quad_ref[3, j]
        before = jnp.where(jnp.logical_and(spots > j, row == target), j, before)
        last = jnp.where(spots == target, j, last)
        return before, last

    row = lax.fori_loop(0, total, targets, none)
    before, last = lax.fori_loop(0, total, link, (none, none))
    links[0:1] = before
    links[1:2] = last
    load_chain = pltpu.make_async_copy(links, chain, chain_sem)
    load_chain.start()
    slots[total] = jnp.zeros((ND, HALO), jnp.float32)

    own.wait()
    load_blocks.wait()
    load_chain.wait()
    for k in steps:
        piece(k, 0, rows, 0).wait_recv()

    def frequency(f):
        return pl.ds(pl.multiple_of(f * ND, ND), ND)

    def take(f, carry):
        value = points_ref[frequency(f)]
        rounded[f] = value.astype(jnp.bfloat16)
        fields[f] = value
        return carry

    lax.fori_loop(0, NF, take, 0, unroll=4)

    def interact(i, carry):
        for b in range(batch):
            j = i * batch + b
            matrix = blocks[j]
            left_term = jnp.dot(matrix, rounded[quad_ref[0, j]], preferred_element_type=jnp.float32)
            right_term = lax.dot_general(
                matrix,
                rounded[quad_ref[1, j]],
                (((0,), (0,)), ((), ())),
                preferred_element_type=jnp.float32,
            )
            products[b] = (left_term * right_term * fields[quad_ref[2, j]]).astype(jnp.bfloat16)
        terms = []
        for b in range(batch):
            j = i * batch + b
            term = jnp.dot(blocks[j], products[b], preferred_element_type=jnp.float32)
            terms.append(term * (strength_ref[j] * source_step))
        for b in range(batch):
            j = i * batch + b
            slots[j] = slots[chain[0, j]] + terms[b]
        return carry

    lax.fori_loop(0, total // batch, interact, 0)

    def finish(f, carry):
        updated[frequency(f)] = fields[f] + slots[chain[1, f]]
        return carry

    lax.fori_loop(0, NF, finish, 0, unroll=4)

    @pl.when(goes_first)
    def _():
        pl.semaphore_wait(turn_sem.at[1], 1)

    column = pl.ds(pl.multiple_of(me * HALO, HALO), HALO)
    homes = []
    for k in order:
        target = lax.rem(me + k, peers)
        home = remote(
            updated.at[pl.ds(pl.multiple_of(target * rows, 8), rows)],
            out_ref.at[:, column],
            home_send.at[k],
            home_recv.at[k],
            {"comp": target},
        )
        home.start()
        homes.append(home)
    own = pltpu.make_async_copy(updated.at[place], out_ref.at[:, column], own_sem)
    own.start()
    to_left, to_right = halo(0, rows, 0)

    @pl.when(has_left)
    def _():
        to_left.wait_send()
        for copy in to_left_sides:
            copy.wait_send()

    @pl.when(has_right)
    def _():
        to_right.wait_send()
        for copy in to_right_sides:
            copy.wait_send()

    own.wait()
    for turn, most in ((goes_first, most_first), (jnp.logical_not(goes_first), most_second)):
        if most < rows:

            @pl.when(turn)
            def _(most=most):
                for k in steps:
                    piece(k, most, rows - most, 1).wait_send()

    for home in homes:
        home.wait()


def advance_waves(
    field, wave_speed, substeps, east, north, neighbours, blocks, quad_index, strength, peers, spaces
):
    rows, width = field.shape
    tiles = width // HALO
    reach = SUB * HALO
    total = blocks.shape[0]
    assert width >= reach and spaces % 2 == 0 and max(total, NF) < HALO
    chunk = chunk_rows(rows)
    block = math.gcd(tiles, 4)
    outer = tiles + 2 * SUB
    window = block + 2 * SUB
    batch = math.gcd(total, 32)
    late_first = min(LATE_FIRST, rows // chunk - 1)
    late_second = min(LATE_SECOND, rows // chunk - 1)
    early = min(EARLY, rows // chunk - late_second)
    angles = (np.arange(ND, dtype=np.float32) + np.float32(0.5)) * np.float32(2.0 * math.pi / ND)
    trig = np.stack([np.cos(angles), np.sin(angles)])
    trig = np.ascontiguousarray(np.broadcast_to(trig[:, :, None], (2, ND, HALO)))
    vmem = pl.BlockSpec(memory_space=pltpu.VMEM)
    whole = pl.BlockSpec(memory_space=pl.ANY)
    return pl.pallas_call(
        functools.partial(wave_kernel, peers, spaces, chunk, block, batch, early, late_first, late_second),
        out_shape=pltpu.VMEM((rows, width), jnp.float32),
        in_specs=[whole] * 10,
        out_specs=vmem,
        scratch_shapes=[
            pltpu.SMEM(wave_speed.shape, jnp.float32),
            pltpu.SMEM(substeps.shape, jnp.int32),
            pltpu.VMEM((2, ND, HALO), jnp.float32),
            pltpu.VMEM((1, width), jnp.float32),
            pltpu.VMEM((1, width), jnp.float32),
            pltpu.VMEM((4, width), jnp.int32),
            pltpu.SMEM(quad_index.shape, jnp.int32),
            pltpu.SMEM(strength.shape, jnp.float32),
            pltpu.SemaphoreType.DMA((8,)),
            pltpu.VMEM((peers * rows, HALO), jnp.float32),
            pltpu.VMEM((rows, width + 2 * reach), jnp.float32),
            pltpu.VMEM((tiles, rows, HALO), jnp.float32),
            pltpu.VMEM((2, 4, reach), jnp.int32),
            pltpu.VMEM((2, 2, 1, reach), jnp.float32),
            pltpu.VMEM((outer, 2, 2 * HALO, 2 * HALO), jnp.bfloat16),
            pltpu.VMEM((2, outer, 8, HALO), jnp.float32),
            pltpu.VMEM((2, window, chunk, HALO), jnp.float32),
            pltpu.VMEM((window, PARTS * chunk, HALO), jnp.bfloat16),
            pltpu.VMEM((2, window, chunk, HALO), jnp.float32),
            pltpu.VMEM((chunk, HALO), jnp.float32),
            pltpu.VMEM((8, HALO), jnp.int32),
            pltpu.SMEM((8, HALO), jnp.int32),
            pltpu.VMEM(blocks.shape, jnp.bfloat16),
            pltpu.VMEM((NF, ND, HALO), jnp.float32),
            pltpu.VMEM((NF, ND, HALO), jnp.bfloat16),
            pltpu.VMEM((batch, ND, HALO), jnp.bfloat16),
            pltpu.VMEM((total + 1, ND, HALO), jnp.float32),
            pltpu.VMEM((peers * rows, HALO), jnp.float32),
            pltpu.SemaphoreType.REGULAR((2,)),
            pltpu.SemaphoreType.DMA,
            pltpu.SemaphoreType.DMA,
            pltpu.SemaphoreType.DMA,
            pltpu.SemaphoreType.DMA((2, 3)),
            pltpu.SemaphoreType.DMA((2, 3)),
            pltpu.SemaphoreType.DMA((2,)),
            pltpu.SemaphoreType.DMA((2, rows // chunk)),
            pltpu.SemaphoreType.DMA((2, peers)),
            pltpu.SemaphoreType.DMA((peers,)),
            pltpu.SemaphoreType.DMA((peers,)),
            pltpu.SemaphoreType.DMA((peers,)),
            pltpu.SemaphoreType.DMA,
            pltpu.SemaphoreType.REGULAR((2,)),
        ],
        compiler_params=pltpu.CompilerParams(collective_id=0, has_side_effects=True),
    )(
        field,
        wave_speed,
        substeps,
        jnp.asarray(trig),
        east.reshape(1, width),
        north.reshape(1, width),
        neighbours,
        quad_index,
        strength,
        blocks,
    )


def store_kernel(new_ref, out_ref, sem):
    copy = pltpu.make_async_copy(new_ref, out_ref, sem)
    copy.start()
    copy.wait()


def store(new):
    return pl.pallas_call(
        store_kernel,
        out_shape=jax.ShapeDtypeStruct(new.shape, new.dtype),
        in_specs=[pl.BlockSpec(memory_space=pltpu.VMEM)],
        out_specs=pl.BlockSpec(memory_space=pl.ANY),
        scratch_shapes=[pltpu.SemaphoreType.DMA],
        compiler_params=pltpu.CompilerParams(vmem_limit_bytes=1 << 20),
    )(new)


def shards(
    spectrum,
    wave_speed,
    current_east,
    current_north,
    substeps,
    neighbours,
    blocks,
    quad_index,
    strength,
):
    peers = lax.axis_size("comp")
    spaces = lax.axis_size("space")
    rows, width = spectrum.shape
    assert width == peers * HALO
    new = advance_waves(
        spectrum,
        wave_speed,
        substeps,
        current_east,
        current_north,
        neighbours,
        blocks,
        quad_index,
        strength,
        peers,
        spaces,
    )
    return store(new)


def solution(mesh):
    in_specs = (
        P("comp", ("grp", "space")),
        P(),
        P(("grp", "space")),
        P(("grp", "space")),
        P(),
        P(None, ("grp", "space")),
        P(),
        P(),
        P(),
    )
    out_specs = P("comp", ("grp", "space"))
    return jax.shard_map(shards, mesh=mesh, in_specs=in_specs, out_specs=out_specs, check_vma=False)
```

```python
import functools
import math

import jax
import jax.numpy as jnp
import numpy as np
from jax import lax
from jax.experimental import pallas as pl
from jax.experimental.pallas import tpu as pltpu
from jax.sharding import PartitionSpec as P

NF = 36
ND = 64
SUB = 4
HALO = 128
PARTS = 2
EARLY = 2
LATE_FIRST = 2
LATE_SECOND = 4

courant_scale = 0.4
courant_limit = 0.45
source_step = 0.1

MESH = pl.DeviceIdType.MESH


def chunk_rows(rows):
    for size in (64, 72, 48, 32, 24, 16, 8):
        if rows % size == 0:
            return size
    return rows


def greet(peers, spaces):
    me = lax.axis_index("comp")
    here = lax.axis_index("space")
    barrier = pltpu.get_barrier_semaphore()
    count = 0
    for axis, place, size in (("comp", me, peers), ("space", here, spaces)):
        for step, near in ((-1, place > 0), (1, place < size - 1)):

            @pl.when(near)
            def _(axis=axis, place=place, step=step):
                pl.semaphore_signal(
                    barrier, inc=1, device_id={axis: place + step}, device_id_type=MESH
                )

            count = count + jnp.where(near, 1, 0)
    return barrier, count


def pass_word(peers, word_sem):
    me = lax.axis_index("comp")

    def onward(side, waits, step):
        @pl.when(waits)
        def _():
            pl.semaphore_wait(word_sem.at[side], 1)

        pl.semaphore_signal(
            word_sem.at[side], inc=1, device_id={"comp": me + step}, device_id_type=MESH
        )

    def up():
        onward(0, me > 1, 1)

    def down():
        onward(1, me < peers - 2, -1)

    inside = jnp.logical_and(me > 0, me < peers - 1)

    @pl.when(jnp.logical_and(inside, me < peers // 2))
    def _():
        up()
        down()

    @pl.when(jnp.logical_and(inside, me >= peers // 2))
    def _():
        down()
        up()


def hear_word(peers, word_sem):
    me = lax.axis_index("comp")
    if peers > 2:
        for side, last in ((1, me == 0), (0, me == peers - 1)):

            @pl.when(last)
            def _(side=side):
                pl.semaphore_wait(word_sem.at[side], 1)


def send_orders(peers):
    orders = []
    for me in range(peers):
        low = me < peers // 2
        others = [t for t in range(peers) if t != me]
        across = sorted((t for t in others if (t < peers // 2) != low), key=lambda t: -abs(t - me))
        beside = sorted((t for t in others if (t < peers // 2) == low), key=lambda t: abs(t - me))
        inner = me in (peers // 2 - 1, peers // 2)
        row = across + beside if inner else beside + across
        orders.append([(t - me) % peers for t in row])
    return orders


def wave_kernel(
    peers,
    spaces,
    chunk,
    block,
    batch,
    early,
    late_first,
    late_second,
    field_ref,
    wave_in,
    substeps_in,
    trig_in,
    east_in,
    north_in,
    neighbour_in,
    quad_in,
    strength_in,
    blocks_ref,
    out_ref,
    wave_ref,
    substeps_ref,
    trig_ref,
    east_ref,
    north_ref,
    neighbour_ref,
    quad_ref,
    strength_ref,
    small_sem,
    points_ref,
    extended,
    finals,
    side_table,
    side_current,
    selector,
    currents,
    states,
    parts,
    speeds,
    repeats,
    links,
    chain,
    blocks,
    fields,
    rounded,
    products,
    slots,
    updated,
    word_sem,
    load_sem,
    blocks_sem,
    chain_sem,
    side_send,
    side_recv,
    halo_send,
    halo_recv,
    piece_send,
    piece_recv,
    home_send,
    home_recv,
    own_sem,
    turn_sem,
):
    me = lax.axis_index("comp")
    here = lax.axis_index("space")
    rows, width = field_ref.shape
    tiles = width // HALO
    reach = SUB * HALO
    chunks = rows // chunk
    has_left = here > 0
    has_right = here < spaces - 1
    odd = lax.rem(here, 2)
    goes_first = odd == jnp.where(here < spaces // 2, 0, 1)

    barrier, greetings = greet(peers, spaces)
    pairs = (
        (neighbour_in, neighbour_ref),
        (east_in, east_ref),
        (north_in, north_ref),
        (trig_in, trig_ref),
        (substeps_in, substeps_ref),
        (wave_in, wave_ref),
        (quad_in, quad_ref),
        (strength_in, strength_ref),
    )
    loads = [
        pltpu.make_async_copy(source, target, small_sem.at[i])
        for i, (source, target) in enumerate(pairs)
    ]
    for copy in loads:
        copy.start()
    load = pltpu.make_async_copy(field_ref, extended.at[:, pl.ds(reach, width)], load_sem)
    load.start()
    load_blocks = pltpu.make_async_copy(blocks_ref, blocks, blocks_sem)
    load_blocks.start()

    lane = lax.broadcasted_iota(jnp.int32, (4, HALO), 1)
    for side, missing in ((0, jnp.logical_not(has_left)), (1, jnp.logical_not(has_right))):

        @pl.when(missing)
        def _(side=side):
            first = (tiles - SUB) * HALO if side == 0 else 0
            for i in range(SUB):
                part = pl.ds(i * HALO, HALO)
                side_table[side, :, part] = lane + (first + (i + 1) * HALO)
            side_current[side] = jnp.zeros((2, 1, reach), jnp.float32)
            depth = HALO if tiles == block else reach
            start = reach - depth if side == 0 else reach + width

            def clear(g, carry):
                at = pl.ds(pl.multiple_of(g * 8, 8), 8)
                extended[at, pl.ds(start, depth)] = jnp.zeros((8, depth), jnp.float32)
                return carry

            lax.fori_loop(0, rows // 8, clear, 0, unroll=8 if rows % 64 == 0 else 1)

    def spread(row):
        return jnp.broadcast_to(row, (8, HALO))

    spot = lax.broadcasted_iota(jnp.int32, (2 * HALO, HALO), 0)

    def fill(e, table_ref, east_row, north_row, tile, place):
        for d in range(4):
            wanted = table_ref[d : d + 1, place] - (tile + d % 2) * HALO
            half = d // 2 * HALO
            chosen = jnp.where(spot == wanted, 1.0, 0.0).astype(jnp.bfloat16)
            selector[e, d % 2, :, half : half + HALO] = chosen
        currents[0, e] = spread(east_row[:, place])
        currents[1, e] = spread(north_row[:, place])

    def fill_own(j, carry):
        fill(j + SUB, neighbour_ref, east_ref, north_ref, j, pl.ds(pl.multiple_of(j * HALO, HALO), HALO))
        return carry

    for copy in loads[:3]:
        copy.wait()
    lax.fori_loop(0, tiles, fill_own, 0)

    pl.semaphore_wait(barrier, greetings)

    left = {"space": jnp.maximum(here - 1, 0)}
    right = {"space": jnp.minimum(here + 1, spaces - 1)}

    def remote(source, target, send, recv, device):
        return pltpu.make_async_remote_copy(
            src_ref=source,
            dst_ref=target,
            send_sem=send,
            recv_sem=recv,
            device_id=device,
            device_id_type=MESH,
        )

    def sides():
        copies = []
        for side, start, device in ((1, 0, left), (0, width - reach, right)):
            part = pl.ds(start, reach)
            pairs = (
                (neighbour_in.at[:, part], side_table.at[side]),
                (east_in.at[:, part], side_current.at[side, 0]),
                (north_in.at[:, part], side_current.at[side, 1]),
            )
            copies.append(
                [
                    remote(source, target, side_send.at[side, i], side_recv.at[side, i], device)
                    for i, (source, target) in enumerate(pairs)
                ]
            )
        return copies

    def halo(first, count, sem):
        part = pl.ds(first, count)
        to_left = remote(
            field_ref.at[part, pl.ds(0, reach)],
            extended.at[part, pl.ds(reach + width, reach)],
            halo_send.at[1],
            halo_recv.at[1, sem],
            left,
        )
        to_right = remote(
            field_ref.at[part, pl.ds(width - reach, reach)],
            extended.at[part, pl.ds(0, reach)],
            halo_send.at[0],
            halo_recv.at[0, sem],
            right,
        )
        return to_left, to_right

    def rows_of(c):
        return pl.multiple_of(c * chunk, 8)

    to_left_sides, to_right_sides = sides()

    @pl.when(has_left)
    def _():
        for copy in to_left_sides:
            copy.start()

    @pl.when(has_right)
    def _():
        for copy in to_right_sides:
            copy.start()

    def start_halo(c, carry):
        to_left, to_right = halo(rows_of(c), chunk, c)

        @pl.when(has_left)
        def _():
            to_left.start()

        @pl.when(has_right)
        def _():
            to_right.start()

        return carry

    lax.fori_loop(0, chunks, start_halo, 0)
    pass_word(peers, word_sem)

    @pl.when(has_right)
    def _():
        for copy in to_left_sides:
            copy.wait_recv()

    @pl.when(has_left)
    def _():
        for copy in to_right_sides:
            copy.wait_recv()

    trimmed = tiles == block

    @pl.when(jnp.logical_or(has_left, not trimmed))
    def _():
        for i in range(1, SUB):
            place = pl.ds(i * HALO, HALO)
            east_row, north_row = side_current.at[0, 0], side_current.at[0, 1]
            fill(i, side_table.at[0], east_row, north_row, tiles - SUB + i, place)

    @pl.when(jnp.logical_or(has_right, not trimmed))
    def _():
        for i in range(SUB - 1):
            place = pl.ds(i * HALO, HALO)
            east_row, north_row = side_current.at[1, 0], side_current.at[1, 1]
            fill(SUB + tiles + i, side_table.at[1], east_row, north_row, i, place)

    sublane = lax.broadcasted_iota(jnp.int32, (8, HALO), 0)
    window = block + 2 * SUB

    def prepare(first, base, low, high):
        def per_group(g, carry):
            at = pl.ds(pl.multiple_of(g * 8, 8), 8)
            component = me * rows + first + g * 8
            speed = wave_ref[component // ND]
            turn = pl.ds(pl.multiple_of(lax.rem(component, ND), 8), 8)
            own_x = trig_ref[0, turn, :] * speed
            own_y = trig_ref[1, turn, :] * speed
            taken = jnp.full((8, HALO), substeps_ref[component], jnp.int32)
            for i in range(1, 8):
                taken = jnp.where(sublane == i, substeps_ref[component + i], taken)
            count = taken.astype(jnp.float32)
            repeats[at] = count
            scale = courant_scale / count
            for i in range(low, high):
                along_x = (own_x + currents[0, base + i]) * scale
                along_y = (own_y + currents[1, base + i]) * scale
                speeds[0, i, at] = jnp.clip(along_x, -courant_limit, courant_limit)
                speeds[1, i, at] = jnp.clip(along_y, -courant_limit, courant_limit)
            return carry

        lax.fori_loop(0, chunk // 8, per_group, 0)

    stacked = chunk % 16 == 0

    def pick(i, chosen):
        if stacked:
            pair = jnp.concatenate([parts[i], parts[i + 1]], axis=1)
            both = jnp.dot(pair, chosen, preferred_element_type=jnp.float32)
            taken = both[:chunk]
            for p in range(1, PARTS):
                taken = taken + both[p * chunk : (p + 1) * chunk]
        else:
            taken = None
            for p in range(PARTS):
                at = pl.ds(p * chunk, chunk)
                pair = jnp.concatenate([parts[i, at], parts[i + 1, at]], axis=1)
                term = jnp.dot(pair, chosen, preferred_element_type=jnp.float32)
                taken = term if taken is None else taken + term
        return taken[:, :HALO], taken[:, HALO:]

    def advance(first, b, open_left=True, open_right=True):
        base = b * block
        at = pl.ds(first, chunk)
        low = 0 if open_left else SUB - 1
        high = window if open_right else window - SUB + 1
        prepare(first, base, low + 1, high - 1)

        def state(s, i):
            if s == 0:
                return extended[at, pl.ds(pl.multiple_of((base + i) * HALO, HALO), HALO)]
            return states[s % 2, i]

        for s in range(SUB):
            edge = min(s, 1)
            for i in range(max(s, low + edge), min(window - s, high - edge)):
                rest = state(s, i)
                for p in range(PARTS):
                    part = rest.astype(jnp.bfloat16)
                    parts[i, p * chunk : (p + 1) * chunk] = part
                    if p + 1 < PARTS:
                        rest = rest - part.astype(jnp.float32)
            for i in range(max(s, low) + 1, min(window - s, high) - 1):
                value = state(s, i)
                west, south = pick(i - 1, selector[base + i, 0])
                east, north = pick(i, selector[base + i, 1])
                along_x = speeds[0, i]
                along_y = speeds[1, i]
                change = jnp.abs(along_x) * (value - jnp.where(along_x > 0.0, west, east))
                change = change + jnp.abs(along_y) * (
                    value - jnp.where(along_y > 0.0, south, north)
                )
                if s > 0:
                    change = jnp.where(repeats[...] > float(s), change, 0.0)
                if s + 1 < SUB:
                    states[(s + 1) % 2, i] = value - change
                else:
                    finals[base + i - SUB, at] = value - change

    def piece(k, first, count, group):
        target = lax.rem(me + k, peers)
        return remote(
            finals.at[target, pl.ds(first, count)],
            points_ref.at[pl.ds(pl.multiple_of(me * rows + first, 8), count)],
            piece_send.at[group, k],
            piece_recv.at[k],
            {"comp": target},
        )

    orders = send_orders(peers)
    order = []
    for place in range(peers - 1):
        k = orders[0][place]
        for other in range(1, peers):
            k = jnp.where(me == other, orders[other][place], k)
        order.append(k)
    steps = range(1, peers)
    for copy in loads[3:]:
        copy.wait()
    load.wait()

    late = jnp.where(goes_first, late_first, late_second)

    def step(c, carry):
        first = rows_of(c)
        to_left, to_right = halo(first, chunk, c)

        @pl.when(has_right)
        def _():
            to_left.wait_recv()

        @pl.when(has_left)
        def _():
            to_right.wait_recv()

        def per_block(b, inner):
            advance(first, b)
            return inner

        if trimmed:

            @pl.when(jnp.logical_and(has_left, has_right))
            def _():
                advance(first, 0)

            @pl.when(jnp.logical_not(has_left))
            def _():
                advance(first, 0, open_left=False)

            @pl.when(jnp.logical_not(has_right))
            def _():
                advance(first, 0, open_right=False)

        else:
            lax.fori_loop(0, tiles // block, per_block, 0)

        @pl.when(c == 0)
        def _():
            hear_word(peers, word_sem)

        @pl.when(jnp.logical_or(goes_first, c < early))
        def _():
            for k in order:
                piece(k, first, chunk, jnp.where(c < chunks - late, 0, 1)).start()

        return carry

    lax.fori_loop(0, chunks, step, 0)
    place = pl.ds(pl.multiple_of(me * rows, 8), rows)
    own = pltpu.make_async_copy(finals.at[me], points_ref.at[place], own_sem)
    own.start()
    most_first = (chunks - late_first) * chunk
    most_second = (chunks - late_second) * chunk
    partner = {"space": here + 1 - 2 * odd}

    @pl.when(goes_first)
    def _():
        for k in steps:
            piece(k, 0, most_first, 0).wait_send()
        pl.semaphore_signal(turn_sem.at[0], inc=1, device_id=partner, device_id_type=MESH)

    @pl.when(jnp.logical_not(goes_first))
    def _():
        pl.semaphore_wait(turn_sem.at[0], 1)
        if early * chunk < most_second:
            for k in order:
                piece(k, early * chunk, most_second - early * chunk, 0).start()
        if late_second:
            for k in order:
                piece(k, most_second, rows - most_second, 1).start()
        for k in steps:
            piece(k, 0, most_second, 0).wait_send()
        pl.semaphore_signal(turn_sem.at[1], inc=1, device_id=partner, device_id_type=MESH)

    total = blocks.shape[0]
    spots = lax.broadcasted_iota(jnp.int32, (1, HALO), 1)
    none = jnp.full((1, HALO), total, jnp.int32)

    def targets(j, row):
        return jnp.where(spots == j, quad_ref[3, j], row)

    def link(j, carry):
        before, last = carry
        target = quad_ref[3, j]
        before = jnp.where(jnp.logical_and(spots > j, row == target), j, before)
        last = jnp.where(spots == target, j, last)
        return before, last

    row = lax.fori_loop(0, total, targets, none)
    before, last = lax.fori_loop(0, total, link, (none, none))
    links[0:1] = before
    links[1:2] = last
    load_chain = pltpu.make_async_copy(links, chain, chain_sem)
    load_chain.start()
    slots[total] = jnp.zeros((ND, HALO), jnp.float32)

    own.wait()
    load_blocks.wait()
    load_chain.wait()
    for k in steps:
        piece(k, 0, rows, 0).wait_recv()

    def frequency(f):
        return pl.ds(pl.multiple_of(f * ND, ND), ND)

    def take(f, carry):
        value = points_ref[frequency(f)]
        rounded[f] = value.astype(jnp.bfloat16)
        fields[f] = value
        return carry

    lax.fori_loop(0, NF, take, 0, unroll=4)

    def interact(i, carry):
        for b in range(batch):
            j = i * batch + b
            matrix = blocks[j]
            left_term = jnp.dot(matrix, rounded[quad_ref[0, j]], preferred_element_type=jnp.float32)
            right_term = lax.dot_general(
                matrix,
                rounded[quad_ref[1, j]],
                (((0,), (0,)), ((), ())),
                preferred_element_type=jnp.float32,
            )
            products[b] = (left_term * right_term * fields[quad_ref[2, j]]).astype(jnp.bfloat16)
        terms = []
        for b in range(batch):
            j = i * batch + b
            term = jnp.dot(blocks[j], products[b], preferred_element_type=jnp.float32)
            terms.append(term * (strength_ref[j] * source_step))
        for b in range(batch):
            j = i * batch + b
            slots[j] = slots[chain[0, j]] + terms[b]
        return carry

    lax.fori_loop(0, total // batch, interact, 0)

    def finish(f, carry):
        updated[frequency(f)] = fields[f] + slots[chain[1, f]]
        return carry

    lax.fori_loop(0, NF, finish, 0, unroll=4)

    @pl.when(goes_first)
    def _():
        pl.semaphore_wait(turn_sem.at[1], 1)

    column = pl.ds(pl.multiple_of(me * HALO, HALO), HALO)
    homes = []
    for k in order:
        target = lax.rem(me + k, peers)
        home = remote(
            updated.at[pl.ds(pl.multiple_of(target * rows, 8), rows)],
            out_ref.at[:, column],
            home_send.at[k],
            home_recv.at[k],
            {"comp": target},
        )
        home.start()
        homes.append(home)
    own = pltpu.make_async_copy(updated.at[place], out_ref.at[:, column], own_sem)
    own.start()
    to_left, to_right = halo(0, rows, 0)

    @pl.when(has_left)
    def _():
        to_left.wait_send()
        for copy in to_left_sides:
            copy.wait_send()

    @pl.when(has_right)
    def _():
        to_right.wait_send()
        for copy in to_right_sides:
            copy.wait_send()

    own.wait()
    for turn, most in ((goes_first, most_first), (jnp.logical_not(goes_first), most_second)):
        if most < rows:

            @pl.when(turn)
            def _(most=most):
                for k in steps:
                    piece(k, most, rows - most, 1).wait_send()

    for home in homes:
        home.wait()


def advance_waves(
    field, wave_speed, substeps, east, north, neighbours, blocks, quad_index, strength, peers, spaces
):
    rows, width = field.shape
    tiles = width // HALO
    reach = SUB * HALO
    total = blocks.shape[0]
    assert width >= reach and spaces % 2 == 0 and max(total, NF) < HALO
    chunk = chunk_rows(rows)
    block = math.gcd(tiles, 4)
    outer = tiles + 2 * SUB
    window = block + 2 * SUB
    batch = math.gcd(total, 32)
    late_first = min(LATE_FIRST, rows // chunk - 1)
    late_second = min(LATE_SECOND, rows // chunk - 1)
    early = min(EARLY, rows // chunk - late_second)
    angles = (np.arange(ND, dtype=np.float32) + np.float32(0.5)) * np.float32(2.0 * math.pi / ND)
    trig = np.stack([np.cos(angles), np.sin(angles)])
    trig = np.ascontiguousarray(np.broadcast_to(trig[:, :, None], (2, ND, HALO)))
    vmem = pl.BlockSpec(memory_space=pltpu.VMEM)
    whole = pl.BlockSpec(memory_space=pl.ANY)
    return pl.pallas_call(
        functools.partial(wave_kernel, peers, spaces, chunk, block, batch, early, late_first, late_second),
        out_shape=pltpu.VMEM((rows, width), jnp.float32),
        in_specs=[whole] * 10,
        out_specs=vmem,
        scratch_shapes=[
            pltpu.SMEM(wave_speed.shape, jnp.float32),
            pltpu.SMEM(substeps.shape, jnp.int32),
            pltpu.VMEM((2, ND, HALO), jnp.float32),
            pltpu.VMEM((1, width), jnp.float32),
            pltpu.VMEM((1, width), jnp.float32),
            pltpu.VMEM((4, width), jnp.int32),
            pltpu.SMEM(quad_index.shape, jnp.int32),
            pltpu.SMEM(strength.shape, jnp.float32),
            pltpu.SemaphoreType.DMA((8,)),
            pltpu.VMEM((peers * rows, HALO), jnp.float32),
            pltpu.VMEM((rows, width + 2 * reach), jnp.float32),
            pltpu.VMEM((tiles, rows, HALO), jnp.float32),
            pltpu.VMEM((2, 4, reach), jnp.int32),
            pltpu.VMEM((2, 2, 1, reach), jnp.float32),
            pltpu.VMEM((outer, 2, 2 * HALO, 2 * HALO), jnp.bfloat16),
            pltpu.VMEM((2, outer, 8, HALO), jnp.float32),
            pltpu.VMEM((2, window, chunk, HALO), jnp.float32),
            pltpu.VMEM((window, PARTS * chunk, HALO), jnp.bfloat16),
            pltpu.VMEM((2, window, chunk, HALO), jnp.float32),
            pltpu.VMEM((chunk, HALO), jnp.float32),
            pltpu.VMEM((8, HALO), jnp.int32),
            pltpu.SMEM((8, HALO), jnp.int32),
            pltpu.VMEM(blocks.shape, jnp.bfloat16),
            pltpu.VMEM((NF, ND, HALO), jnp.float32),
            pltpu.VMEM((NF, ND, HALO), jnp.bfloat16),
            pltpu.VMEM((batch, ND, HALO), jnp.bfloat16),
            pltpu.VMEM((total + 1, ND, HALO), jnp.float32),
            pltpu.VMEM((peers * rows, HALO), jnp.float32),
            pltpu.SemaphoreType.REGULAR((2,)),
            pltpu.SemaphoreType.DMA,
            pltpu.SemaphoreType.DMA,
            pltpu.SemaphoreType.DMA,
            pltpu.SemaphoreType.DMA((2, 3)),
            pltpu.SemaphoreType.DMA((2, 3)),
            pltpu.SemaphoreType.DMA((2,)),
            pltpu.SemaphoreType.DMA((2, rows // chunk)),
            pltpu.SemaphoreType.DMA((2, peers)),
            pltpu.SemaphoreType.DMA((peers,)),
            pltpu.SemaphoreType.DMA((peers,)),
            pltpu.SemaphoreType.DMA((peers,)),
            pltpu.SemaphoreType.DMA,
            pltpu.SemaphoreType.REGULAR((2,)),
        ],
        compiler_params=pltpu.CompilerParams(collective_id=0, has_side_effects=True),
    )(
        field,
        wave_speed,
        substeps,
        jnp.asarray(trig),
        east.reshape(1, width),
        north.reshape(1, width),
        neighbours,
        quad_index,
        strength,
        blocks,
    )


def store_kernel(new_ref, out_ref, sem):
    copy = pltpu.make_async_copy(new_ref, out_ref, sem)
    copy.start()
    copy.wait()


def store(new):
    return pl.pallas_call(
        store_kernel,
        out_shape=jax.ShapeDtypeStruct(new.shape, new.dtype),
        in_specs=[pl.BlockSpec(memory_space=pltpu.VMEM)],
        out_specs=pl.BlockSpec(memory_space=pl.ANY),
        scratch_shapes=[pltpu.SemaphoreType.DMA],
        compiler_params=pltpu.CompilerParams(vmem_limit_bytes=1 << 20),
    )(new)


def shards(
    spectrum,
    wave_speed,
    current_east,
    current_north,
    substeps,
    neighbours,
    blocks,
    quad_index,
    strength,
):
    peers = lax.axis_size("comp")
    spaces = lax.axis_size("space")
    rows, width = spectrum.shape
    assert width == peers * HALO
    new = advance_waves(
        spectrum,
        wave_speed,
        substeps,
        current_east,
        current_north,
        neighbours,
        blocks,
        quad_index,
        strength,
        peers,
        spaces,
    )
    return store(new)


def solution(mesh):
    in_specs = (
        P("comp", ("grp", "space")),
        P(),
        P(("grp", "space")),
        P(("grp", "space")),
        P(),
        P(None, ("grp", "space")),
        P(),
        P(),
        P(),
    )
    out_specs = P("comp", ("grp", "space"))
    return jax.shard_map(shards, mesh=mesh, in_specs=in_specs, out_specs=out_specs, check_vma=False)
```
